32 devices in a mesh: slab: 2 (over y), seq: 4 (over z), head: 4 (over x, core).
Axes of the slice: x: 2, y: 2, z: 4, core: 2. Of those that a mesh axis runs over, the one named last changes fastest.
Arguments:
- values_first: bfloat16 [4, 1024, 1024], P('slab', 'seq', 'head'), parts along dimension 0, may hold values from -6 to 6
- keys_first: bfloat16 [4, 1024, 1024], P('slab', 'seq', 'head'), parts along dimension 0, may hold values from -0.5 to 0.5
- queries_first: bfloat16 [4, 1024, 1024], P('slab', 'seq', 'head'), parts along dimension 0, may hold values from -0.5 to 0.5
- steps_first: float32 [4, 8, 1024], P('slab', 'head', 'seq'), parts along dimension 0, may hold values from 0 to 0.35
- rates_first: float32 [8], P('head'), may hold values from 1 to 2
- skip_first: float32 [8], P('head'), may hold values from 1 to 4
- gain_first: float32 [1024], P('head'), may hold values from 0.5 to 1.5
- w_values: bfloat16 [8, 128, 128], P('head'), may hold values from -0.5 to 0.5
- w_keys: bfloat16 [8, 128, 256], P('head'), may hold values from -0.046875 to 0.046875
- w_step: bfloat16 [8, 128], P('head'), may hold values from -0.5 to 0.5
- step_bias: float32 [8], P('head'), may hold values from -1 to 1
- rates_second: float32 [8], P('head'), may hold values from 0 to 0.04
- skip_second: float32 [8], P('head'), may hold values from 1 to 4
- gain_second: float32 [1024], P('head'), may hold values from 0.5 to 1.5
Outputs:
- mixed: bfloat16 [4, 1024, 1024], P('slab', 'seq', 'head'), parts along dimension 0
The draws below stay inside these ranges and needn't reach their ends.
There are 2 independent parts, one for each index of `slab`. The reference program is written for one: setup_inputs(seed, part) draws one part's arguments, and reference() takes and returns one part's arrays. A program takes and returns all parts, laid end to end along the dimension named above; an argument that names none is the same for every part. Nothing has to cross between parts.
All inputs are finite; a program needn't handle non-finite values.
Results may differ from the reference program's by a relative error of at most 0.007.
Values may be sent and summed in bfloat16 or wider, within the bound.
A program may use at most 64 MiB of HBM per device.

```python
import math
import jax
import jax.numpy as jnp
from jax import lax

ATTN_UNIT_COUNT = 8
P_SIZE = 128
N = 128
BLOCK = 256
BATCH_PLATES = 2
GR = 32
GC = 32
TILE_SERIES = 1024
TOK_DEV = 256


def draw_steps_first(key, part):
    key_order, key_base, key_place, lookup_extent = jax.random.split(key, 4)
    ranking = jax.random.permutation(key_order, ATTN_UNIT_COUNT)
    keeping = ATTN_UNIT_COUNT // 2
    slow_heads = (ranking < keeping)[None, :, None]
    initial_speed = jax.random.uniform(key_base, (BATCH_PLATES, ATTN_UNIT_COUNT, TILE_SERIES), jnp.float32, 0.5, 1.5)
    tile_locations = jax.random.randint(key_place, (BATCH_PLATES, ATTN_UNIT_COUNT, 2), 0, TILE_SERIES)
    tile_location_index = lax.broadcasted_iota(jnp.int32, (BATCH_PLATES, ATTN_UNIT_COUNT, TILE_SERIES), 2)
    segment_bundles = jnp.logical_or(tile_location_index == tile_locations[:, :, 0:1], tile_location_index == tile_locations[:, :, 1:2])
    segment_extent = jax.random.uniform(lookup_extent, (BATCH_PLATES, ATTN_UNIT_COUNT, 1), jnp.float32, 0.25, 0.35)
    lagging_increments = jnp.where(segment_bundles, segment_extent, initial_speed * (0.4 / TILE_SERIES))
    return jnp.where(slow_heads, lagging_increments, initial_speed * 0.025)


def draw_rates_second(key, part):
    key_order, key_slow, key_fast = jax.random.split(key, 3)
    ranking = jax.random.permutation(key_order, ATTN_UNIT_COUNT)
    keeping = ATTN_UNIT_COUNT // 2
    slow_heads = ranking < keeping
    slow_rate = jax.random.uniform(key_slow, (ATTN_UNIT_COUNT,), jnp.float32, 0.5, 1.0) * (0.3 / TILE_SERIES)
    fast_rate = jnp.exp(jax.random.uniform(key_fast, (ATTN_UNIT_COUNT,), jnp.float32, jnp.log(0.02), jnp.log(0.04)))
    return jnp.where(slow_heads, slow_rate, fast_rate)


def level_of(stream_key, dims, cuts, least, largest):
    level = 1.0
    for position, parts in cuts:
        heights = jax.random.uniform(jax.random.fold_in(jax.random.fold_in(stream_key, 6), position), (parts,), jnp.float32, least / len(cuts), largest / len(cuts))
        level = level * jnp.repeat(jnp.exp(heights), dims[position] // parts).reshape((-1,) + (1,) * (len(dims) - 1 - position))
    return level


def centred(key, shape, scale, bound, pieces=(), held_as=jnp.bfloat16):
    level = level_of(key, shape, pieces, -0.22, 0.18) if pieces else 1.0
    array = jax.random.normal(key, shape, jnp.float32) * scale * level
    return jnp.minimum(jnp.maximum(array, -bound), bound).astype(held_as)


def setup_inputs(seed: int = 0, part: int = 0) -> dict:
    splits = jax.random.split(jax.random.key(seed), 15)
    part_splits = jax.random.split(jax.random.fold_in(splits[14], part), 15)
    values_first = centred(part_splits[0], (BATCH_PLATES, TILE_SERIES, ATTN_UNIT_COUNT * P_SIZE), 1.0, 6.0, ((1, 4), (2, 4)))
    keys_first = centred(part_splits[1], (BATCH_PLATES, TILE_SERIES, ATTN_UNIT_COUNT * N), N ** -0.5, 0.5, ((1, 4), (2, 4)))
    queries_first = centred(part_splits[2], (BATCH_PLATES, TILE_SERIES, ATTN_UNIT_COUNT * N), N ** -0.5, 0.5, ((1, 4), (2, 4)))
    steps_first = draw_steps_first(jax.random.fold_in(jax.random.fold_in(splits[14], part), 71), part)
    rates_first = jnp.clip(jnp.exp(math.log(2.0) - 0.6931472 * jax.random.uniform(splits[4], (ATTN_UNIT_COUNT,), jnp.float32) ** level_of(splits[4], (ATTN_UNIT_COUNT,), ((0, 4),), -0.2, 0.2)), 1.0, 2.0)
    skip_first = jnp.clip(jnp.exp(math.log(4.0) - 1.3862944 * jax.random.uniform(splits[5], (ATTN_UNIT_COUNT,), jnp.float32) ** level_of(splits[5], (ATTN_UNIT_COUNT,), ((0, 4),), -0.2, 0.2)), 1.0, 4.0)
    gain_first = jnp.clip(1.0 + 0.1 * jax.random.normal(splits[6], (ATTN_UNIT_COUNT * P_SIZE,), jnp.float32), 0.5, 1.5)
    w_values = centred(splits[7], (ATTN_UNIT_COUNT, P_SIZE, P_SIZE), P_SIZE ** -0.5, 0.5, ((0, 4),))
    w_keys = centred(splits[8], (ATTN_UNIT_COUNT, P_SIZE, 2 * N), (P_SIZE * N) ** -0.5, 0.046875, ((0, 4),))
    w_step = centred(splits[9], (ATTN_UNIT_COUNT, P_SIZE), P_SIZE ** -0.5, 0.5, ((0, 4),))
    step_bias = jnp.clip(jax.random.uniform(splits[10], (ATTN_UNIT_COUNT,), jnp.float32, -1.0, 1.0) * level_of(splits[10], (ATTN_UNIT_COUNT,), ((0, 4),), -0.4, 0.0), -1.0, 1.0)
    rates_second = draw_rates_second(jax.random.fold_in(splits[14], 71), part)
    skip_second = jnp.clip(jnp.exp(math.log(4.0) - 1.3862944 * jax.random.uniform(splits[12], (ATTN_UNIT_COUNT,), jnp.float32) ** level_of(splits[12], (ATTN_UNIT_COUNT,), ((0, 4),), -0.2, 0.2)), 1.0, 4.0)
    gain_second = jnp.clip(1.0 + 0.1 * jax.random.normal(splits[13], (ATTN_UNIT_COUNT * P_SIZE,), jnp.float32), 0.5, 1.5)
    return {"values_first": values_first, "keys_first": keys_first, "queries_first": queries_first, "steps_first": steps_first, "rates_first": rates_first, "skip_first": skip_first, "gain_first": gain_first, "w_values": w_values, "w_keys": w_keys, "w_step": w_step, "step_bias": step_bias, "rates_second": rates_second, "skip_second": skip_second, "gain_second": gain_second}


def rounded(values):
    return lax.optimization_barrier(values.astype(jnp.bfloat16)).astype(jnp.float32)

def reference_scan(values, keys_in, queries, log_decay, skip, gain):
    length = values.shape[0]
    block_len = min(BLOCK, TOK_DEV)
    blocks = length // block_len
    value_blocks = values.astype(jnp.float32).reshape(blocks, block_len, ATTN_UNIT_COUNT, P_SIZE)
    key_blocks = keys_in.astype(jnp.float32).reshape(blocks, block_len, ATTN_UNIT_COUNT, N)
    query_blocks = queries.astype(jnp.float32).reshape(blocks, block_len, ATTN_UNIT_COUNT, N)
    log_blocks = jnp.transpose(log_decay.astype(jnp.float32).reshape(ATTN_UNIT_COUNT, blocks, block_len), (1, 0, 2))
    row_ids = lax.broadcasted_iota(jnp.int32, (block_len, block_len), 0)
    col_ids = lax.broadcasted_iota(jnp.int32, (block_len, block_len), 1)

    def advance(carried, entry_item):
        value_block, key_block, query_block, log_block = entry_item
        running = jnp.cumsum(log_block, axis=1)
        scores = jnp.einsum('ihn,jhn->hij', query_block, key_block, precision=lax.Precision.HIGHEST)
        spread = running[:, :, None] - running[:, None, :]
        decays = jnp.exp(jnp.where(row_ids >= col_ids, spread, -jnp.inf))
        mixing = rounded(scores * decays)
        inner_sum = jnp.einsum('hij,jhp->ihp', mixing, value_block, precision=lax.Precision.HIGHEST)
        outer_sum = jnp.einsum('ihn,hnp->ihp', query_block, rounded(carried), precision=lax.Precision.HIGHEST)
        raw_out = inner_sum + outer_sum * jnp.exp(running).T[:, :, None] + skip[None, :, None] * value_block
        scaled = raw_out * lax.rsqrt(lax.optimization_barrier(jnp.mean(raw_out * raw_out, axis=-1, keepdims=True)) + 1e-05)
        normed = (scaled * gain.reshape(ATTN_UNIT_COUNT, P_SIZE)[None]).astype(jnp.bfloat16)
        to_end = jnp.exp(running[:, -1:] - running)
        weighted = rounded(key_block * to_end.T[:, :, None])
        local_state = jnp.einsum('jhn,jhp->hnp', weighted, value_block, precision=lax.Precision.HIGHEST)
        updated = jnp.exp(running[:, -1])[:, None, None] * carried + local_state
        return (updated, normed)
    final_state, normed_all = lax.scan(advance, jnp.zeros((ATTN_UNIT_COUNT, N, P_SIZE), jnp.float32), (value_blocks, key_blocks, query_blocks, log_blocks))
    return normed_all.reshape(length, ATTN_UNIT_COUNT * P_SIZE)

def reference(values_first, keys_first, queries_first, steps_first, rates_first, skip_first, gain_first, w_values, w_keys, w_step, step_bias, rates_second, skip_second, gain_second):

    def one_slab(entry_item):
        values_one, keys_one, queries_one, steps_one = entry_item
        first_out = reference_scan(values_one, keys_one, queries_one, -rates_first[:, None] * steps_one, skip_first, gain_first)
        columns = jnp.transpose(first_out.reshape(GR, GC, ATTN_UNIT_COUNT, P_SIZE), (1, 0, 2, 3)).reshape(TILE_SERIES, ATTN_UNIT_COUNT, P_SIZE).astype(jnp.float32)
        values_two = rounded(jnp.einsum('lhp,hpk->lhk', columns, w_values.astype(jnp.float32), precision=lax.Precision.HIGHEST))
        keys_two = rounded(jnp.einsum('lhp,hpk->lhk', columns, w_keys.astype(jnp.float32), precision=lax.Precision.HIGHEST))
        step_pre = rounded(jnp.einsum('lhp,hp->hl', columns, w_step.astype(jnp.float32), precision=lax.Precision.HIGHEST))
        steps_two = jax.nn.softplus(step_pre + step_bias[:, None])
        second_out = reference_scan(values_two.reshape(TILE_SERIES, ATTN_UNIT_COUNT * P_SIZE), keys_two[:, :, :N].reshape(TILE_SERIES, ATTN_UNIT_COUNT * N), keys_two[:, :, N:].reshape(TILE_SERIES, ATTN_UNIT_COUNT * N), -rates_second[:, None] * steps_two, skip_second, gain_second)
        second_home = jnp.transpose(second_out.reshape(GC, GR, ATTN_UNIT_COUNT * P_SIZE), (1, 0, 2)).reshape(TILE_SERIES, ATTN_UNIT_COUNT * P_SIZE)
        return (first_out.astype(jnp.float32) + second_home.astype(jnp.float32)).astype(jnp.bfloat16)
    return lax.map(one_slab, (values_first, keys_first, queries_first, steps_first))
```

```python
import functools
import math

import jax
import jax.numpy as jnp
from jax import lax
from jax.experimental import pallas as pl
from jax.experimental.pallas import tpu as pltpu
from jax.sharding import PartitionSpec as P

N = 128
BLOCK = 256
ROWS_DEV = 8


def block_terms(values, keys_in, queries, log_decay, block_len):
    slab_count, length, feat_width = values.shape
    head_count = log_decay.shape[1]
    blocks = length // block_len
    value_blocks = values.reshape(
        slab_count, blocks, block_len, head_count, feat_width // head_count
    )
    key_blocks = keys_in.reshape(
        slab_count, blocks, block_len, head_count, keys_in.shape[2] // head_count
    )
    query_blocks = queries.reshape(
        slab_count, blocks, block_len, head_count, queries.shape[2] // head_count
    )
    running = jnp.cumsum(log_decay.reshape(slab_count, head_count, blocks, block_len), axis=3)
    running_sc = jnp.transpose(running, (0, 2, 1, 3))
    running_pos = jnp.transpose(running, (0, 2, 3, 1))
    scores = jnp.einsum(
        "scihn,scjhn->schij", query_blocks, key_blocks, preferred_element_type=jnp.float32
    )
    row_ids = lax.broadcasted_iota(jnp.int32, (block_len, block_len), 0)
    col_ids = lax.broadcasted_iota(jnp.int32, (block_len, block_len), 1)
    spread = running_sc[..., :, None] - running_sc[..., None, :]
    decays = jnp.exp(jnp.where(row_ids >= col_ids, spread, -jnp.inf))
    mixing = (scores * decays).astype(jnp.bfloat16)
    inner_sum = jnp.einsum(
        "schij,scjhp->scihp", mixing, value_blocks, preferred_element_type=jnp.float32
    )
    to_end = jnp.exp(running_pos[:, :, -1:, :] - running_pos)
    weighted = (key_blocks * to_end[..., None]).astype(jnp.bfloat16)
    local_states = jnp.einsum(
        "scjhn,scjhp->schnp", weighted, value_blocks, preferred_element_type=jnp.float32
    )
    block_logs = running_sc[..., -1]
    return (value_blocks, query_blocks, running_pos, inner_sum, local_states, block_logs)


def entry_states(local_states, block_logs):

    def advance(carried, entry_item):
        update, log_total = entry_item
        return (jnp.exp(log_total)[..., None, None] * carried + update, carried)

    start_state = jnp.zeros(local_states.shape[:1] + local_states.shape[2:], jnp.float32)
    final_state, entries = lax.scan(
        advance, start_state, (jnp.moveaxis(local_states, 1, 0), jnp.moveaxis(block_logs, 1, 0))
    )
    return (final_state, jnp.moveaxis(entries, 0, 1))


def carry_into(final_state, device_log):
    log_totals = lax.all_gather(device_log[None], "seq", axis=0, tiled=True)
    my_index = lax.axis_index("seq")
    ranks_all = lax.iota(jnp.int32, log_totals.shape[0])
    between = jnp.logical_and(
        ranks_all[None, :] > ranks_all[:, None], ranks_all[None, :] < my_index
    ).astype(jnp.float32)
    span_logs = jnp.einsum("dk,ksh->dsh", between, log_totals, precision=lax.Precision.HIGHEST)
    weights = jnp.where((ranks_all < my_index)[:, None, None], jnp.exp(span_logs), 0.0)
    return jnp.sum(
        weights[..., None, None] * lax.all_gather(final_state[None], "seq", axis=0, tiled=True),
        axis=0,
    )


def selective_scan(values, keys_in, queries, log_decay, skip, gain):
    block_len = min(BLOCK, values.shape[1])
    value_blocks, query_blocks, running_pos, inner_sum, local_states, block_logs = block_terms(
        values, keys_in, queries, log_decay, block_len
    )
    final_state, entries = entry_states(local_states, block_logs)
    carried = carry_into(final_state, jnp.sum(block_logs, axis=1))
    before = jnp.cumsum(block_logs, axis=1) - block_logs
    states = (entries + jnp.exp(before)[..., None, None] * carried[:, None]).astype(jnp.bfloat16)
    outer_sum = jnp.einsum(
        "scihn,schnp->scihp", query_blocks, states, preferred_element_type=jnp.float32
    )
    raw_out = (
        inner_sum
        + outer_sum * jnp.exp(running_pos)[..., None]
        + skip[:, None] * value_blocks.astype(jnp.float32)
    )
    scaled = raw_out * lax.rsqrt(jnp.mean(raw_out * raw_out, axis=-1, keepdims=True) + 1e-05)
    normed = (scaled * gain.reshape(skip.shape[0], -1)).astype(jnp.bfloat16)
    return normed.reshape(normed.shape[0], -1, normed.shape[3] * normed.shape[4])


def project_rows(features, w_values, w_keys, w_step):
    slab_count, length, feat_width = features.shape
    head_count = w_values.shape[0]
    split_feat = features.reshape(slab_count, length, head_count, feat_width // head_count)
    values_two = jnp.einsum(
        "slhp,hpk->slhk", split_feat, w_values, preferred_element_type=jnp.float32
    ).astype(jnp.bfloat16)
    keys_two = jnp.einsum(
        "slhp,hpk->slhk", split_feat, w_keys, preferred_element_type=jnp.float32
    ).astype(jnp.bfloat16)
    step_pre = jnp.einsum(
        "slhp,hp->slh", split_feat, w_step, preferred_element_type=jnp.float32
    ).astype(jnp.bfloat16)
    return (values_two, keys_two, step_pre)


def second_scan(values_two, keys_two, step_pre, step_bias, rates_second, skip_second, gain_second):
    slab_count, length, head_count, key_width = keys_two.shape
    step_size = jax.nn.softplus(step_pre.astype(jnp.float32) + step_bias)
    log_decay = -rates_second[None, :, None] * jnp.transpose(step_size, (0, 2, 1))
    return selective_scan(
        values_two.reshape(slab_count, length, -1),
        keys_two[..., :N].reshape(slab_count, length, -1),
        keys_two[..., N:].reshape(slab_count, length, -1),
        log_decay,
        skip_second,
        gain_second,
    )


def columns_from(received):
    slab_count, rows_all, cols_here, last_width = received.shape
    return jnp.transpose(received, (0, 2, 1, 3)).reshape(
        slab_count, cols_here * rows_all, last_width
    )


def local(
    values_first,
    keys_first,
    queries_first,
    steps_first,
    rates_first,
    skip_first,
    gain_first,
    w_values,
    w_keys,
    w_step,
    step_bias,
    rates_second,
    skip_second,
    gain_second,
):
    log_first = -rates_first[None, :, None] * steps_first
    first_out = selective_scan(
        values_first, keys_first, queries_first, log_first, skip_first, gain_first
    )
    slab_count, length, feat_width = first_out.shape
    home_grid = first_out.reshape(slab_count, ROWS_DEV, length // ROWS_DEV, feat_width)
    received = lax.all_to_all(home_grid, "seq", split_axis=2, concat_axis=1, tiled=True)
    rows_all = received.shape[1]
    cols_here = received.shape[2]
    values_two, keys_two, step_pre = project_rows(columns_from(received), w_values, w_keys, w_step)
    result = second_scan(
        values_two, keys_two, step_pre, step_bias, rates_second, skip_second, gain_second
    )
    column_out = result.reshape(received.shape[0], cols_here, rows_all, result.shape[2])
    home_back = lax.all_to_all(column_out, "seq", split_axis=2, concat_axis=1, tiled=True)
    second_home = jnp.transpose(home_back, (0, 2, 1, 3)).reshape(slab_count, length, feat_width)
    return (first_out.astype(jnp.float32) + second_home.astype(jnp.float32)).astype(jnp.bfloat16)


def cumsum_rows(rows, upper):
    high = rows.astype(jnp.bfloat16).astype(jnp.float32)
    rest = rows - high
    mid = rest.astype(jnp.bfloat16).astype(jnp.float32)
    low = rest - mid
    count = rows.shape[0]
    stacked = jnp.concatenate([high, mid, low, jnp.zeros_like(low)], axis=0).astype(jnp.bfloat16)
    sums = jnp.dot(stacked, upper, preferred_element_type=jnp.float32)
    return sums[:count] + sums[count : 2 * count] + sums[2 * count : 3 * count]


def dot_nt(left, right):
    return lax.dot_general(
        left, right, (((1,), (1,)), ((), ())), preferred_element_type=jnp.float32
    )


def dot_tn(left, right):
    return lax.dot_general(
        left, right, (((0,), (0,)), ((), ())), preferred_element_type=jnp.float32
    )


def scan_block(values, keys_in, queries, run_row, state, skip, gain):
    length, width = values.shape
    half = length // 2
    run_col = jnp.transpose(jnp.broadcast_to(run_row, (width, length)))
    lower = lax.broadcasted_iota(jnp.int32, (half, half), 0) >= lax.broadcasted_iota(
        jnp.int32, (half, half), 1
    )
    reps = half // width

    def decay(rows, columns, masked):
        left = jnp.concatenate([run_col[rows]] * reps, axis=1) if reps > 1 else run_col[rows]
        spread = left - run_row[:, columns]
        return jnp.exp(jnp.where(lower, spread, -jnp.inf) if masked else spread)

    top, bottom = slice(0, half), slice(half, length)
    scores_top = dot_nt(queries[top], keys_in[top])
    scores_bottom = dot_nt(queries[bottom], keys_in)
    mix_top = (scores_top * decay(top, top, True)).astype(jnp.bfloat16)
    mix_bottom = jnp.concatenate(
        [
            (scores_bottom[:, top] * decay(bottom, top, False)).astype(jnp.bfloat16),
            (scores_bottom[:, bottom] * decay(bottom, bottom, True)).astype(jnp.bfloat16),
        ],
        axis=1,
    )
    inner = jnp.concatenate(
        [
            jnp.dot(mix_top, values[top], preferred_element_type=jnp.float32),
            jnp.dot(mix_bottom, values, preferred_element_type=jnp.float32),
        ],
        axis=0,
    )
    raw = inner + skip * values.astype(jnp.float32)
    if state is not None:
        outer = jnp.dot(queries, state.astype(jnp.bfloat16), preferred_element_type=jnp.float32)
        raw = raw + jnp.exp(run_col) * outer
    mean_sq = jnp.mean(raw * raw, axis=1, keepdims=True)
    normed = (raw * lax.rsqrt(mean_sq + 1e-05) * gain).astype(jnp.bfloat16)
    last = run_col[length - 1 : length, :]
    weighted = (keys_in.astype(jnp.float32) * jnp.exp(last - run_col)).astype(jnp.bfloat16)
    update = dot_tn(weighted, values)
    if state is not None:
        update = update + jnp.exp(last) * state
    return normed, update


def fused_kernel(
    parts,
    heads,
    values,
    keys_in,
    queries,
    steps,
    w_values,
    w_keys,
    w_step,
    gain_first,
    gain_second,
    rates_first,
    skip_first,
    step_bias,
    rates_second,
    skip_second,
    out,
    v_buf,
    k_buf,
    q_buf,
    step_buf,
    wv_buf,
    wk_buf,
    first_buf,
    turn_buf,
    send_buf,
    own_sem,
    in_send,
    in_recv,
    out_own,
    out_send,
    out_recv,
):
    me = lax.axis_index("seq")
    length, width = v_buf.shape[1:]
    rows_all, cols_here = send_buf.shape[1:3]
    rows_here = rows_all // parts
    my_slab, my_head = me // heads, lax.rem(me, heads)

    def lanes(head):
        return pl.ds(pl.multiple_of(head * width, width), width)

    def pieces(owner):
        slab, head = owner // heads, lax.rem(owner, heads)
        return (
            steps.at[slab],
            keys_in.at[slab, :, lanes(head)],
            queries.at[slab, :, lanes(head)],
            values.at[slab, :, lanes(head)],
        )

    landing = (step_buf, k_buf, q_buf, v_buf)

    barrier = pltpu.get_barrier_semaphore()
    for hop in range(1, parts):
        pl.semaphore_signal(
            barrier,
            inc=1,
            device_id={"seq": lax.rem(me + hop, parts)},
            device_id_type=pl.DeviceIdType.MESH,
        )
    own = [
        pltpu.make_async_copy(src, dst.at[me], own_sem.at[kind])
        for kind, (src, dst) in enumerate(zip(pieces(me), landing))
    ]
    own.append(pltpu.make_async_copy(w_values.at[my_head], wv_buf, own_sem.at[len(landing)]))
    own.append(pltpu.make_async_copy(w_keys.at[my_head], wk_buf, own_sem.at[len(landing) + 1]))
    for copy in own:
        copy.start()
    pl.semaphore_wait(barrier, parts - 1)

    sends = []
    for hop in range(1, parts):
        target = lax.rem(me + hop, parts)
        for kind, (src, dst) in enumerate(zip(pieces(target), landing)):
            copy = pltpu.make_async_remote_copy(
                src_ref=src,
                dst_ref=dst.at[me],
                send_sem=in_send.at[kind, hop],
                recv_sem=in_recv.at[kind, me],
                device_id={"seq": target},
                device_id_type=pl.DeviceIdType.MESH,
            )
            copy.start()
            sends.append(copy)

    def await_block(source, kinds):
        for kind in kinds:
            src, dst = pieces(me)[kind], landing[kind]
            pltpu.make_async_remote_copy(
                src_ref=src,
                dst_ref=dst.at[source],
                send_sem=in_send.at[kind, 0],
                recv_sem=in_recv.at[kind, source],
                device_id={"seq": source},
                device_id_type=pl.DeviceIdType.MESH,
            ).wait_recv()

    upper = jnp.where(
        lax.broadcasted_iota(jnp.int32, (length, length), 0)
        <= lax.broadcasted_iota(jnp.int32, (length, length), 1),
        1.0,
        0.0,
    ).astype(jnp.bfloat16)

    def pick(ref, axis_size, select):
        chosen = select(0)
        for head in range(1, axis_size):
            chosen = jnp.where(my_head == head, select(head), chosen)
        return chosen

    gain_one = pick(gain_first, heads, lambda h: gain_first[:, h * width : (h + 1) * width])
    gain_two = pick(gain_second, heads, lambda h: gain_second[:, h * width : (h + 1) * width])
    step_row = pick(w_step, heads, lambda h: w_step[...].astype(jnp.float32)[h : h + 1, :])
    step_rows = jnp.broadcast_to(step_row, (16, width)).astype(jnp.bfloat16)
    skip_one, skip_two = skip_first[my_head], skip_second[my_head]

    for copy in own:
        copy.wait()

    state = None
    for block in range(parts):
        @pl.when(me != block)
        def _():
            await_block(block, range(len(landing)))

        log_row = -rates_first[my_head] * step_buf[block, pl.ds(my_head, 1), :]
        run_row = cumsum_rows(jnp.broadcast_to(log_row, (8, length)), upper)[0:1]
        normed, state = scan_block(
            v_buf[block], k_buf[block], q_buf[block], run_row, state, skip_one, gain_one
        )
        first_buf[pl.ds(block * length, length), :] = normed.astype(jnp.float32)

    state = None
    for block in range(parts):
        columns = jnp.concatenate(
            [
                first_buf[pl.ds(block * cols_here + col, rows_all, stride=rows_all), :]
                for col in range(cols_here)
            ],
            axis=0,
        ).astype(jnp.bfloat16)
        values_two = jnp.dot(
            columns, wv_buf[...], preferred_element_type=jnp.float32
        ).astype(jnp.bfloat16)
        keys_two = jnp.dot(columns, wk_buf[...], preferred_element_type=jnp.float32).astype(
            jnp.bfloat16
        )
        pre = dot_nt(step_rows, columns)[0:8].astype(jnp.bfloat16).astype(jnp.float32)
        shifted = pre + step_bias[my_head]
        soft = jnp.maximum(shifted, 0.0) + jnp.log1p(jnp.exp(-jnp.abs(shifted)))
        run_row = cumsum_rows(-rates_second[my_head] * soft, upper)[0:1]
        half = keys_two.shape[1] // 2
        normed, state = scan_block(
            values_two, keys_two[:, :half], keys_two[:, half:], run_row, state, skip_two, gain_two
        )
        turn_buf[block] = normed.astype(jnp.float32)
        for row in range(rows_all):
            total = (
                first_buf[pl.ds(row * rows_all + block * cols_here, cols_here), :]
                + turn_buf[block, pl.ds(row, cols_here, stride=rows_all), :]
            )
            send_buf[block, row] = total.astype(jnp.bfloat16)

        def home(owner):
            return send_buf.at[block, pl.ds(owner * rows_here, rows_here)]

        def place(owner):
            slab, head = owner // heads, lax.rem(owner, heads)
            return out.at[slab, :, pl.ds(block * cols_here, cols_here), lanes(head)]

        for hop in range(1, parts):
            target = lax.rem(me + hop, parts)
            copy = pltpu.make_async_remote_copy(
                src_ref=home(target),
                dst_ref=place(me),
                send_sem=out_send.at[block, hop],
                recv_sem=out_recv.at[block, me],
                device_id={"seq": target},
                device_id_type=pl.DeviceIdType.MESH,
            )
            copy.start()
            sends.append(copy)
        pltpu.make_async_copy(home(me), place(me), out_own.at[block]).start()

    for block in range(parts):
        def place(owner):
            slab, head = owner // heads, lax.rem(owner, heads)
            return out.at[slab, :, pl.ds(block * cols_here, cols_here), lanes(head)]

        mine = send_buf.at[block, pl.ds(me * rows_here, rows_here)]
        pltpu.make_async_copy(mine, place(me), out_own.at[block]).wait()
        for hop in range(1, parts):
            source = lax.rem(me + hop, parts)
            pltpu.make_async_remote_copy(
                src_ref=mine,
                dst_ref=place(source),
                send_sem=out_send.at[block, 0],
                recv_sem=out_recv.at[block, source],
                device_id={"seq": source},
                device_id_type=pl.DeviceIdType.MESH,
            ).wait_recv()
    for copy in sends:
        copy.wait_send()


def local_fused(
    parts,
    values_first,
    keys_first,
    queries_first,
    steps_first,
    rates_first,
    skip_first,
    gain_first,
    w_values,
    w_keys,
    w_step,
    step_bias,
    rates_second,
    skip_second,
    gain_second,
):
    slab_count, length, feat_width = values_first.shape
    heads = rates_first.shape[0]
    width = feat_width // heads
    grid_side = math.isqrt(parts * length)
    rows_here, cols_here = grid_side // parts, length // grid_side
    anywhere = pl.BlockSpec(memory_space=pl.ANY)
    vmem = pl.BlockSpec(memory_space=pltpu.VMEM)
    smem = pl.BlockSpec(memory_space=pltpu.SMEM)
    dma = pltpu.SemaphoreType.DMA
    mixed = pl.pallas_call(
        functools.partial(fused_kernel, parts, heads),
        out_shape=jax.ShapeDtypeStruct(
            (slab_count, rows_here, grid_side, feat_width), jnp.bfloat16
        ),
        in_specs=[anywhere] * 6 + [vmem] * 3 + [smem] * 5,
        out_specs=anywhere,
        scratch_shapes=[
            pltpu.VMEM((parts, length, width), jnp.bfloat16),
            pltpu.VMEM((parts, length, width), jnp.bfloat16),
            pltpu.VMEM((parts, length, width), jnp.bfloat16),
            pltpu.VMEM((parts, heads, length), jnp.float32),
            pltpu.VMEM(w_values.shape[1:], jnp.bfloat16),
            pltpu.VMEM(w_keys.shape[1:], jnp.bfloat16),
            pltpu.VMEM((parts * length, width), jnp.float32),
            pltpu.VMEM((parts, length, width), jnp.float32),
            pltpu.VMEM((parts, grid_side, cols_here, width), jnp.bfloat16),
            dma((6,)),
            dma((4, parts)),
            dma((4, parts)),
            dma((parts,)),
            dma((parts, parts)),
            dma((parts, parts)),
        ],
        compiler_params=pltpu.CompilerParams(collective_id=0, has_side_effects=True),
    )(
        values_first,
        keys_first,
        queries_first,
        steps_first,
        w_values,
        w_keys,
        w_step,
        gain_first.reshape(1, -1),
        gain_second.reshape(1, -1),
        rates_first,
        skip_first,
        step_bias,
        rates_second,
        skip_second,
    )
    return mixed.reshape(values_first.shape)


def fits_fused(parts, args):
    values, w_values, w_keys = args[0], args[7], args[8]
    slab_count, length, feat_width = values.shape
    heads = args[4].shape[0]
    side = math.isqrt(parts * length)
    return (
        slab_count * heads == parts
        and length <= BLOCK
        and length % 256 == 0
        and side * side == parts * length
        and side % parts == 0
        and length % side == 0
        and (length // side) % 8 == 0
        and feat_width // heads == 128
        and w_values.shape[1:] == (128, 128)
        and w_keys.shape[1:] == (128, 256)
    )


def solution(mesh):
    parts = mesh.shape["seq"]

    def chosen(*args):
        if fits_fused(parts, args):
            return local_fused(parts, *args)
        return local(*args)

    placed = (
        P("slab", "seq", "head"),
        P("slab", "seq", "head"),
        P("slab", "seq", "head"),
        P("slab", "head", "seq"),
        P("head"),
        P("head"),
        P("head"),
        P("head", None, None),
        P("head", None, None),
        P("head", None),
        P("head"),
        P("head"),
        P("head"),
        P("head"),
    )
    return jax.shard_map(
        chosen, mesh=mesh, in_specs=placed, out_specs=P("slab", "seq", "head"), check_vma=False
    )
```

```python
import functools
import math

import jax
import jax.numpy as jnp
from jax import lax
from jax.experimental import pallas as pl
from jax.experimental.pallas import tpu as pltpu
from jax.sharding import PartitionSpec as P

N = 128
BLOCK = 256
ROWS_DEV = 8
VMEM_GRANT = 16 << 20


def block_terms(values, keys_in, queries, log_decay, block_len):
    slab_count, length, feat_width = values.shape
    head_count = log_decay.shape[1]
    blocks = length // block_len
    value_blocks = values.reshape(
        slab_count, blocks, block_len, head_count, feat_width // head_count
    )
    key_blocks = keys_in.reshape(
        slab_count, blocks, block_len, head_count, keys_in.shape[2] // head_count
    )
    query_blocks = queries.reshape(
        slab_count, blocks, block_len, head_count, queries.shape[2] // head_count
    )
    running = jnp.cumsum(log_decay.reshape(slab_count, head_count, blocks, block_len), axis=3)
    running_sc = jnp.transpose(running, (0, 2, 1, 3))
    running_pos = jnp.transpose(running, (0, 2, 3, 1))
    scores = jnp.einsum(
        "scihn,scjhn->schij", query_blocks, key_blocks, preferred_element_type=jnp.float32
    )
    row_ids = lax.broadcasted_iota(jnp.int32, (block_len, block_len), 0)
    col_ids = lax.broadcasted_iota(jnp.int32, (block_len, block_len), 1)
    spread = running_sc[..., :, None] - running_sc[..., None, :]
    decays = jnp.exp(jnp.where(row_ids >= col_ids, spread, -jnp.inf))
    mixing = (scores * decays).astype(jnp.bfloat16)
    inner_sum = jnp.einsum(
        "schij,scjhp->scihp", mixing, value_blocks, preferred_element_type=jnp.float32
    )
    to_end = jnp.exp(running_pos[:, :, -1:, :] - running_pos)
    weighted = (key_blocks * to_end[..., None]).astype(jnp.bfloat16)
    local_states = jnp.einsum(
        "scjhn,scjhp->schnp", weighted, value_blocks, preferred_element_type=jnp.float32
    )
    block_logs = running_sc[..., -1]
    return (value_blocks, query_blocks, running_pos, inner_sum, local_states, block_logs)


def entry_states(local_states, block_logs):

    def advance(carried, entry_item):
        update, log_total = entry_item
        return (jnp.exp(log_total)[..., None, None] * carried + update, carried)

    start_state = jnp.zeros(local_states.shape[:1] + local_states.shape[2:], jnp.float32)
    final_state, entries = lax.scan(
        advance, start_state, (jnp.moveaxis(local_states, 1, 0), jnp.moveaxis(block_logs, 1, 0))
    )
    return (final_state, jnp.moveaxis(entries, 0, 1))


def carry_into(final_state, device_log):
    log_totals = lax.all_gather(device_log[None], "seq", axis=0, tiled=True)
    my_index = lax.axis_index("seq")
    ranks_all = lax.iota(jnp.int32, log_totals.shape[0])
    between = jnp.logical_and(
        ranks_all[None, :] > ranks_all[:, None], ranks_all[None, :] < my_index
    ).astype(jnp.float32)
    span_logs = jnp.einsum("dk,ksh->dsh", between, log_totals, precision=lax.Precision.HIGHEST)
    weights = jnp.where((ranks_all < my_index)[:, None, None], jnp.exp(span_logs), 0.0)
    return jnp.sum(
        weights[..., None, None] * lax.all_gather(final_state[None], "seq", axis=0, tiled=True),
        axis=0,
    )


def selective_scan(values, keys_in, queries, log_decay, skip, gain):
    block_len = min(BLOCK, values.shape[1])
    value_blocks, query_blocks, running_pos, inner_sum, local_states, block_logs = block_terms(
        values, keys_in, queries, log_decay, block_len
    )
    final_state, entries = entry_states(local_states, block_logs)
    carried = carry_into(final_state, jnp.sum(block_logs, axis=1))
    before = jnp.cumsum(block_logs, axis=1) - block_logs
    states = (entries + jnp.exp(before)[..., None, None] * carried[:, None]).astype(jnp.bfloat16)
    outer_sum = jnp.einsum(
        "scihn,schnp->scihp", query_blocks, states, preferred_element_type=jnp.float32
    )
    raw_out = (
        inner_sum
        + outer_sum * jnp.exp(running_pos)[..., None]
        + skip[:, None] * value_blocks.astype(jnp.float32)
    )
    scaled = raw_out * lax.rsqrt(jnp.mean(raw_out * raw_out, axis=-1, keepdims=True) + 1e-05)
    normed = (scaled * gain.reshape(skip.shape[0], -1)).astype(jnp.bfloat16)
    return normed.reshape(normed.shape[0], -1, normed.shape[3] * normed.shape[4])


def project_rows(features, w_values, w_keys, w_step):
    slab_count, length, feat_width = features.shape
    head_count = w_values.shape[0]
    split_feat = features.reshape(slab_count, length, head_count, feat_width // head_count)
    values_two = jnp.einsum(
        "slhp,hpk->slhk", split_feat, w_values, preferred_element_type=jnp.float32
    ).astype(jnp.bfloat16)
    keys_two = jnp.einsum(
        "slhp,hpk->slhk", split_feat, w_keys, preferred_element_type=jnp.float32
    ).astype(jnp.bfloat16)
    step_pre = jnp.einsum(
        "slhp,hp->slh", split_feat, w_step, preferred_element_type=jnp.float32
    ).astype(jnp.bfloat16)
    return (values_two, keys_two, step_pre)


def second_scan(values_two, keys_two, step_pre, step_bias, rates_second, skip_second, gain_second):
    slab_count, length, head_count, key_width = keys_two.shape
    step_size = jax.nn.softplus(step_pre.astype(jnp.float32) + step_bias)
    log_decay = -rates_second[None, :, None] * jnp.transpose(step_size, (0, 2, 1))
    return selective_scan(
        values_two.reshape(slab_count, length, -1),
        keys_two[..., :N].reshape(slab_count, length, -1),
        keys_two[..., N:].reshape(slab_count, length, -1),
        log_decay,
        skip_second,
        gain_second,
    )


def columns_from(received):
    slab_count, rows_all, cols_here, last_width = received.shape
    return jnp.transpose(received, (0, 2, 1, 3)).reshape(
        slab_count, cols_here * rows_all, last_width
    )


def local(
    values_first,
    keys_first,
    queries_first,
    steps_first,
    rates_first,
    skip_first,
    gain_first,
    w_values,
    w_keys,
    w_step,
    step_bias,
    rates_second,
    skip_second,
    gain_second,
):
    log_first = -rates_first[None, :, None] * steps_first
    first_out = selective_scan(
        values_first, keys_first, queries_first, log_first, skip_first, gain_first
    )
    slab_count, length, feat_width = first_out.shape
    home_grid = first_out.reshape(slab_count, ROWS_DEV, length // ROWS_DEV, feat_width)
    received = lax.all_to_all(home_grid, "seq", split_axis=2, concat_axis=1, tiled=True)
    rows_all = received.shape[1]
    cols_here = received.shape[2]
    values_two, keys_two, step_pre = project_rows(columns_from(received), w_values, w_keys, w_step)
    result = second_scan(
        values_two, keys_two, step_pre, step_bias, rates_second, skip_second, gain_second
    )
    column_out = result.reshape(received.shape[0], cols_here, rows_all, result.shape[2])
    home_back = lax.all_to_all(column_out, "seq", split_axis=2, concat_axis=1, tiled=True)
    second_home = jnp.transpose(home_back, (0, 2, 1, 3)).reshape(slab_count, length, feat_width)
    return (first_out.astype(jnp.float32) + second_home.astype(jnp.float32)).astype(jnp.bfloat16)


def cumsum_rows(rows, upper):
    high = rows.astype(jnp.bfloat16).astype(jnp.float32)
    rest = rows - high
    mid = rest.astype(jnp.bfloat16).astype(jnp.float32)
    low = rest - mid
    count = rows.shape[0]
    stacked = jnp.concatenate([high, mid, low, jnp.zeros_like(low)], axis=0).astype(jnp.bfloat16)
    sums = jnp.dot(stacked, upper, preferred_element_type=jnp.float32)
    return sums[:count] + sums[count : 2 * count] + sums[2 * count : 3 * count]


def dot_nt(left, right):
    return lax.dot_general(
        left, right, (((1,), (1,)), ((), ())), preferred_element_type=jnp.float32
    )


def dot_tn(left, right):
    return lax.dot_general(
        left, right, (((0,), (0,)), ((), ())), preferred_element_type=jnp.float32
    )


def scan_block(values, keys_in, queries, run_row, state, skip, gain):
    length, width = values.shape
    half = length // 2
    run_col = jnp.transpose(jnp.broadcast_to(run_row, (width, length)))
    lower = lax.broadcasted_iota(jnp.int32, (half, half), 0) >= lax.broadcasted_iota(
        jnp.int32, (half, half), 1
    )
    reps = half // width

    def decay(rows, columns, masked):
        left = jnp.concatenate([run_col[rows]] * reps, axis=1) if reps > 1 else run_col[rows]
        spread = left - run_row[:, columns]
        return jnp.exp(jnp.where(lower, spread, -jnp.inf) if masked else spread)

    top, bottom = slice(0, half), slice(half, length)
    scores_top = dot_nt(queries[top], keys_in[top])
    scores_bottom = dot_nt(queries[bottom], keys_in)
    mix_top = (scores_top * decay(top, top, True)).astype(jnp.bfloat16)
    mix_bottom = jnp.concatenate(
        [
            (scores_bottom[:, top] * decay(bottom, top, False)).astype(jnp.bfloat16),
            (scores_bottom[:, bottom] * decay(bottom, bottom, True)).astype(jnp.bfloat16),
        ],
        axis=1,
    )
    inner = jnp.concatenate(
        [
            jnp.dot(mix_top, values[top], preferred_element_type=jnp.float32),
            jnp.dot(mix_bottom, values, preferred_element_type=jnp.float32),
        ],
        axis=0,
    )
    raw = inner + skip * values.astype(jnp.float32)
    if state is not None:
        outer = jnp.dot(queries, state.astype(jnp.bfloat16), preferred_element_type=jnp.float32)
        raw = raw + jnp.exp(run_col) * outer
    mean_sq = jnp.mean(raw * raw, axis=1, keepdims=True)
    normed = (raw * lax.rsqrt(mean_sq + 1e-05) * gain).astype(jnp.bfloat16)
    last = run_col[length - 1 : length, :]
    weighted = (keys_in.astype(jnp.float32) * jnp.exp(last - run_col)).astype(jnp.bfloat16)
    update = dot_tn(weighted, values)
    if state is not None:
        update = update + jnp.exp(last) * state
    return normed, update


def fused_kernel(parts, heads, *refs):
    values, keys_in, queries, steps, w_values, w_keys = refs[:6]
    small_in, out = refs[6:14], refs[14]
    v_buf, k_buf, q_buf, step_buf, wv_buf, wk_buf = refs[15:21]
    small = refs[21:29]
    w_step, gain_first, gain_second = small[:3]
    rates_first, skip_first, step_bias, rates_second, skip_second = small[3:]
    first_buf, turn_buf, send_buf = refs[29:32]
    own_sem, in_send, in_recv, out_own, out_send, out_recv = refs[32:]
    me = lax.axis_index("seq")
    length, width = v_buf.shape[1:]
    rows_all, cols_here = send_buf.shape[1:3]
    rows_here = rows_all // parts
    my_slab, my_head = me // heads, lax.rem(me, heads)

    def lanes(head):
        return pl.ds(pl.multiple_of(head * width, width), width)

    def pieces(owner):
        slab, head = owner // heads, lax.rem(owner, heads)
        return (
            steps.at[slab],
            keys_in.at[slab, :, lanes(head)],
            queries.at[slab, :, lanes(head)],
            values.at[slab, :, lanes(head)],
        )

    landing = (step_buf, k_buf, q_buf, v_buf)
    turn = jnp.where(me < parts // 2, parts - 1, 1)

    def peer(hop):
        return lax.rem(me + turn * hop, parts)

    barrier = pltpu.get_barrier_semaphore()
    for hop in range(1, parts):
        pl.semaphore_signal(
            barrier,
            inc=1,
            device_id={"seq": lax.rem(me + hop, parts)},
            device_id_type=pl.DeviceIdType.MESH,
        )
    own = [
        pltpu.make_async_copy(src, dst.at[me], own_sem.at[kind])
        for kind, (src, dst) in enumerate(zip(pieces(me), landing))
    ]
    own.append(pltpu.make_async_copy(w_values.at[my_head], wv_buf, own_sem.at[len(landing)]))
    own.append(pltpu.make_async_copy(w_keys.at[my_head], wk_buf, own_sem.at[len(landing) + 1]))
    for index, (src, dst) in enumerate(zip(small_in, small)):
        own.append(pltpu.make_async_copy(src, dst, own_sem.at[len(landing) + 2 + index]))
    for copy in own:
        copy.start()
    pl.semaphore_wait(barrier, parts - 1)

    sends = []
    for hop in range(1, parts):
        target = peer(hop)
        for kind, (src, dst) in enumerate(zip(pieces(target), landing)):
            copy = pltpu.make_async_remote_copy(
                src_ref=src,
                dst_ref=dst.at[me],
                send_sem=in_send.at[kind, hop],
                recv_sem=in_recv.at[kind, me],
                device_id={"seq": target},
                device_id_type=pl.DeviceIdType.MESH,
            )
            copy.start()
            sends.append(copy)

    def await_block(source, kinds):
        for kind in kinds:
            src, dst = pieces(me)[kind], landing[kind]
            pltpu.make_async_remote_copy(
                src_ref=src,
                dst_ref=dst.at[source],
                send_sem=in_send.at[kind, 0],
                recv_sem=in_recv.at[kind, source],
                device_id={"seq": source},
                device_id_type=pl.DeviceIdType.MESH,
            ).wait_recv()

    upper = jnp.where(
        lax.broadcasted_iota(jnp.int32, (length, length), 0)
        <= lax.broadcasted_iota(jnp.int32, (length, length), 1),
        1.0,
        0.0,
    ).astype(jnp.bfloat16)

    for copy in own:
        copy.wait()

    def pick(ref, axis_size, select):
        chosen = select(0)
        for head in range(1, axis_size):
            chosen = jnp.where(my_head == head, select(head), chosen)
        return chosen

    gain_one = pick(gain_first, heads, lambda h: gain_first[:, h * width : (h + 1) * width])
    gain_two = pick(gain_second, heads, lambda h: gain_second[:, h * width : (h + 1) * width])
    step_row = pick(w_step, heads, lambda h: w_step[...].astype(jnp.float32)[h : h + 1, :])
    step_rows = jnp.broadcast_to(step_row, (16, width)).astype(jnp.bfloat16)
    skip_one, skip_two = skip_first[my_head], skip_second[my_head]

    state = None
    for block in range(parts):
        @pl.when(me != block)
        def _():
            await_block(block, range(len(landing)))

        log_row = -rates_first[my_head] * step_buf[block, pl.ds(my_head, 1), :]
        run_row = cumsum_rows(jnp.broadcast_to(log_row, (8, length)), upper)[0:1]
        normed, state = scan_block(
            v_buf[block], k_buf[block], q_buf[block], run_row, state, skip_one, gain_one
        )
        first_buf[pl.ds(block * length, length), :] = normed.astype(jnp.float32)

    state = None
    for block in range(parts):
        columns = jnp.concatenate(
            [
                first_buf[pl.ds(block * cols_here + col, rows_all, stride=rows_all), :]
                for col in range(cols_here)
            ],
            axis=0,
        ).astype(jnp.bfloat16)
        values_two = jnp.dot(
            columns, wv_buf[...], preferred_element_type=jnp.float32
        ).astype(jnp.bfloat16)
        keys_two = jnp.dot(columns, wk_buf[...], preferred_element_type=jnp.float32).astype(
            jnp.bfloat16
        )
        pre = dot_nt(step_rows, columns)[0:8].astype(jnp.bfloat16).astype(jnp.float32)
        shifted = pre + step_bias[my_head]
        soft = jnp.maximum(shifted, 0.0) + jnp.log1p(jnp.exp(-jnp.abs(shifted)))
        run_row = cumsum_rows(-rates_second[my_head] * soft, upper)[0:1]
        half = keys_two.shape[1] // 2
        normed, state = scan_block(
            values_two, keys_two[:, :half], keys_two[:, half:], run_row, state, skip_two, gain_two
        )
        turn_buf[block] = normed.astype(jnp.float32)
        for row in range(rows_all):
            total = (
                first_buf[pl.ds(row * rows_all + block * cols_here, cols_here), :]
                + turn_buf[block, pl.ds(row, cols_here, stride=rows_all), :]
            )
            send_buf[block, row] = total.astype(jnp.bfloat16)

        def home(owner):
            return send_buf.at[block, pl.ds(owner * rows_here, rows_here)]

        def place(owner):
            slab, head = owner // heads, lax.rem(owner, heads)
            return out.at[slab, :, pl.ds(block * cols_here, cols_here), lanes(head)]

        for hop in range(1, parts):
            target = peer(hop)
            copy = pltpu.make_async_remote_copy(
                src_ref=home(target),
                dst_ref=place(me),
                send_sem=out_send.at[block, hop],
                recv_sem=out_recv.at[block, me],
                device_id={"seq": target},
                device_id_type=pl.DeviceIdType.MESH,
            )
            copy.start()
            sends.append(copy)
        pltpu.make_async_copy(home(me), place(me), out_own.at[block]).start()

    for block in range(parts):
        def place(owner):
            slab, head = owner // heads, lax.rem(owner, heads)
            return out.at[slab, :, pl.ds(block * cols_here, cols_here), lanes(head)]

        mine = send_buf.at[block, pl.ds(me * rows_here, rows_here)]
        pltpu.make_async_copy(mine, place(me), out_own.at[block]).wait()
        for hop in range(1, parts):
            source = lax.rem(me + hop, parts)
            pltpu.make_async_remote_copy(
                src_ref=mine,
                dst_ref=place(source),
                send_sem=out_send.at[block, 0],
                recv_sem=out_recv.at[block, source],
                device_id={"seq": source},
                device_id_type=pl.DeviceIdType.MESH,
            ).wait_recv()
    for copy in sends:
        copy.wait_send()


def local_fused(
    parts,
    values_first,
    keys_first,
    queries_first,
    steps_first,
    rates_first,
    skip_first,
    gain_first,
    w_values,
    w_keys,
    w_step,
    step_bias,
    rates_second,
    skip_second,
    gain_second,
):
    slab_count, length, feat_width = values_first.shape
    heads = rates_first.shape[0]
    width = feat_width // heads
    grid_side = math.isqrt(parts * length)
    rows_here, cols_here = grid_side // parts, length // grid_side
    anywhere = pl.BlockSpec(memory_space=pl.ANY)
    dma = pltpu.SemaphoreType.DMA
    mixed = pl.pallas_call(
        functools.partial(fused_kernel, parts, heads),
        out_shape=jax.ShapeDtypeStruct(
            (slab_count, rows_here, grid_side, feat_width), jnp.bfloat16
        ),
        in_specs=[anywhere] * 14,
        out_specs=pl.BlockSpec(memory_space=pltpu.VMEM),
        scratch_shapes=[
            pltpu.VMEM((parts, length, width), jnp.bfloat16),
            pltpu.VMEM((parts, length, width), jnp.bfloat16),
            pltpu.VMEM((parts, length, width), jnp.bfloat16),
            pltpu.VMEM((parts, heads, length), jnp.float32),
            pltpu.VMEM(w_values.shape[1:], jnp.bfloat16),
            pltpu.VMEM(w_keys.shape[1:], jnp.bfloat16),
            pltpu.VMEM(w_step.shape, jnp.bfloat16),
            pltpu.VMEM((1, feat_width), jnp.float32),
            pltpu.VMEM((1, feat_width), jnp.float32),
        ]
        + [pltpu.SMEM((heads,), jnp.float32)] * 5
        + [
            pltpu.VMEM((parts * length, width), jnp.float32),
            pltpu.VMEM((parts, length, width), jnp.float32),
            pltpu.VMEM((parts, grid_side, cols_here, width), jnp.bfloat16),
            dma((14,)),
            dma((4, parts)),
            dma((4, parts)),
            dma((parts,)),
            dma((parts, parts)),
            dma((parts, parts)),
        ],
        compiler_params=pltpu.CompilerParams(
            collective_id=0, has_side_effects=True, vmem_limit_bytes=VMEM_GRANT
        ),
    )(
        *(
            pltpu.with_memory_space_constraint(array, pltpu.HBM)
            for array in (
                values_first,
                keys_first,
                queries_first,
                steps_first,
                w_values,
                w_keys,
                w_step,
                gain_first.reshape(1, -1),
                gain_second.reshape(1, -1),
                rates_first,
                skip_first,
                step_bias,
                rates_second,
                skip_second,
            )
        )
    )
    return mixed.reshape(values_first.shape)


def fits_fused(parts, args):
    values, w_values, w_keys = args[0], args[7], args[8]
    slab_count, length, feat_width = values.shape
    heads = args[4].shape[0]
    side = math.isqrt(parts * length)
    return (
        slab_count * heads == parts
        and length <= BLOCK
        and length % 256 == 0
        and side * side == parts * length
        and side % parts == 0
        and length % side == 0
        and (length // side) % 8 == 0
        and feat_width // heads == 128
        and w_values.shape[1:] == (128, 128)
        and w_keys.shape[1:] == (128, 256)
    )


def solution(mesh):
    parts = mesh.shape["seq"]

    def chosen(*args):
        if fits_fused(parts, args):
            return local_fused(parts, *args)
        return local(*args)

    placed = (
        P("slab", "seq", "head"),
        P("slab", "seq", "head"),
        P("slab", "seq", "head"),
        P("slab", "head", "seq"),
        P("head"),
        P("head"),
        P("head"),
        P("head", None, None),
        P("head", None, None),
        P("head", None),
        P("head"),
        P("head"),
        P("head"),
        P("head"),
    )
    return jax.shard_map(
        chosen, mesh=mesh, in_specs=placed, out_specs=P("slab", "seq", "head"), check_vma=False
    )
```

```python
import functools
import math

import jax
import jax.numpy as jnp
from jax import lax
from jax.experimental import pallas as pl
from jax.experimental.pallas import tpu as pltpu
from jax.sharding import PartitionSpec as P

N = 128
BLOCK = 256
ROWS_DEV = 8
VMEM_GRANT = 16 << 20


def block_terms(values, keys_in, queries, log_decay, block_len):
    slab_count, length, feat_width = values.shape
    head_count = log_decay.shape[1]
    blocks = length // block_len
    value_blocks = values.reshape(
        slab_count, blocks, block_len, head_count, feat_width // head_count
    )
    key_blocks = keys_in.reshape(
        slab_count, blocks, block_len, head_count, keys_in.shape[2] // head_count
    )
    query_blocks = queries.reshape(
        slab_count, blocks, block_len, head_count, queries.shape[2] // head_count
    )
    running = jnp.cumsum(log_decay.reshape(slab_count, head_count, blocks, block_len), axis=3)
    running_sc = jnp.transpose(running, (0, 2, 1, 3))
    running_pos = jnp.transpose(running, (0, 2, 3, 1))
    scores = jnp.einsum(
        "scihn,scjhn->schij", query_blocks, key_blocks, preferred_element_type=jnp.float32
    )
    row_ids = lax.broadcasted_iota(jnp.int32, (block_len, block_len), 0)
    col_ids = lax.broadcasted_iota(jnp.int32, (block_len, block_len), 1)
    spread = running_sc[..., :, None] - running_sc[..., None, :]
    decays = jnp.exp(jnp.where(row_ids >= col_ids, spread, -jnp.inf))
    mixing = (scores * decays).astype(jnp.bfloat16)
    inner_sum = jnp.einsum(
        "schij,scjhp->scihp", mixing, value_blocks, preferred_element_type=jnp.float32
    )
    to_end = jnp.exp(running_pos[:, :, -1:, :] - running_pos)
    weighted = (key_blocks * to_end[..., None]).astype(jnp.bfloat16)
    local_states = jnp.einsum(
        "scjhn,scjhp->schnp", weighted, value_blocks, preferred_element_type=jnp.float32
    )
    block_logs = running_sc[..., -1]
    return (value_blocks, query_blocks, running_pos, inner_sum, local_states, block_logs)


def entry_states(local_states, block_logs):

    def advance(carried, entry_item):
        update, log_total = entry_item
        return (jnp.exp(log_total)[..., None, None] * carried + update, carried)

    start_state = jnp.zeros(local_states.shape[:1] + local_states.shape[2:], jnp.float32)
    final_state, entries = lax.scan(
        advance, start_state, (jnp.moveaxis(local_states, 1, 0), jnp.moveaxis(block_logs, 1, 0))
    )
    return (final_state, jnp.moveaxis(entries, 0, 1))


def carry_into(final_state, device_log):
    log_totals = lax.all_gather(device_log[None], "seq", axis=0, tiled=True)
    my_index = lax.axis_index("seq")
    ranks_all = lax.iota(jnp.int32, log_totals.shape[0])
    between = jnp.logical_and(
        ranks_all[None, :] > ranks_all[:, None], ranks_all[None, :] < my_index
    ).astype(jnp.float32)
    span_logs = jnp.einsum("dk,ksh->dsh", between, log_totals, precision=lax.Precision.HIGHEST)
    weights = jnp.where((ranks_all < my_index)[:, None, None], jnp.exp(span_logs), 0.0)
    return jnp.sum(
        weights[..., None, None] * lax.all_gather(final_state[None], "seq", axis=0, tiled=True),
        axis=0,
    )


def selective_scan(values, keys_in, queries, log_decay, skip, gain):
    block_len = min(BLOCK, values.shape[1])
    value_blocks, query_blocks, running_pos, inner_sum, local_states, block_logs = block_terms(
        values, keys_in, queries, log_decay, block_len
    )
    final_state, entries = entry_states(local_states, block_logs)
    carried = carry_into(final_state, jnp.sum(block_logs, axis=1))
    before = jnp.cumsum(block_logs, axis=1) - block_logs
    states = (entries + jnp.exp(before)[..., None, None] * carried[:, None]).astype(jnp.bfloat16)
    outer_sum = jnp.einsum(
        "scihn,schnp->scihp", query_blocks, states, preferred_element_type=jnp.float32
    )
    raw_out = (
        inner_sum
        + outer_sum * jnp.exp(running_pos)[..., None]
        + skip[:, None] * value_blocks.astype(jnp.float32)
    )
    scaled = raw_out * lax.rsqrt(jnp.mean(raw_out * raw_out, axis=-1, keepdims=True) + 1e-05)
    normed = (scaled * gain.reshape(skip.shape[0], -1)).astype(jnp.bfloat16)
    return normed.reshape(normed.shape[0], -1, normed.shape[3] * normed.shape[4])


def project_rows(features, w_values, w_keys, w_step):
    slab_count, length, feat_width = features.shape
    head_count = w_values.shape[0]
    split_feat = features.reshape(slab_count, length, head_count, feat_width // head_count)
    values_two = jnp.einsum(
        "slhp,hpk->slhk", split_feat, w_values, preferred_element_type=jnp.float32
    ).astype(jnp.bfloat16)
    keys_two = jnp.einsum(
        "slhp,hpk->slhk", split_feat, w_keys, preferred_element_type=jnp.float32
    ).astype(jnp.bfloat16)
    step_pre = jnp.einsum(
        "slhp,hp->slh", split_feat, w_step, preferred_element_type=jnp.float32
    ).astype(jnp.bfloat16)
    return (values_two, keys_two, step_pre)


def second_scan(values_two, keys_two, step_pre, step_bias, rates_second, skip_second, gain_second):
    slab_count, length, head_count, key_width = keys_two.shape
    step_size = jax.nn.softplus(step_pre.astype(jnp.float32) + step_bias)
    log_decay = -rates_second[None, :, None] * jnp.transpose(step_size, (0, 2, 1))
    return selective_scan(
        values_two.reshape(slab_count, length, -1),
        keys_two[..., :N].reshape(slab_count, length, -1),
        keys_two[..., N:].reshape(slab_count, length, -1),
        log_decay,
        skip_second,
        gain_second,
    )


def columns_from(received):
    slab_count, rows_all, cols_here, last_width = received.shape
    return jnp.transpose(received, (0, 2, 1, 3)).reshape(
        slab_count, cols_here * rows_all, last_width
    )


def local(
    values_first,
    keys_first,
    queries_first,
    steps_first,
    rates_first,
    skip_first,
    gain_first,
    w_values,
    w_keys,
    w_step,
    step_bias,
    rates_second,
    skip_second,
    gain_second,
):
    log_first = -rates_first[None, :, None] * steps_first
    first_out = selective_scan(
        values_first, keys_first, queries_first, log_first, skip_first, gain_first
    )
    slab_count, length, feat_width = first_out.shape
    home_grid = first_out.reshape(slab_count, ROWS_DEV, length // ROWS_DEV, feat_width)
    received = lax.all_to_all(home_grid, "seq", split_axis=2, concat_axis=1, tiled=True)
    rows_all = received.shape[1]
    cols_here = received.shape[2]
    values_two, keys_two, step_pre = project_rows(columns_from(received), w_values, w_keys, w_step)
    result = second_scan(
        values_two, keys_two, step_pre, step_bias, rates_second, skip_second, gain_second
    )
    column_out = result.reshape(received.shape[0], cols_here, rows_all, result.shape[2])
    home_back = lax.all_to_all(column_out, "seq", split_axis=2, concat_axis=1, tiled=True)
    second_home = jnp.transpose(home_back, (0, 2, 1, 3)).reshape(slab_count, length, feat_width)
    return (first_out.astype(jnp.float32) + second_home.astype(jnp.float32)).astype(jnp.bfloat16)


def cumsum_rows(rows, upper):
    high = rows.astype(jnp.bfloat16).astype(jnp.float32)
    rest = rows - high
    mid = rest.astype(jnp.bfloat16).astype(jnp.float32)
    low = rest - mid
    count = rows.shape[0]
    stacked = jnp.concatenate([high, mid, low, jnp.zeros_like(low)], axis=0).astype(jnp.bfloat16)
    sums = jnp.dot(stacked, upper, preferred_element_type=jnp.float32)
    return sums[:count] + sums[count : 2 * count] + sums[2 * count : 3 * count]


def dot_nt(left, right):
    return lax.dot_general(
        left, right, (((1,), (1,)), ((), ())), preferred_element_type=jnp.float32
    )


def dot_tn(left, right):
    return lax.dot_general(
        left, right, (((0,), (0,)), ((), ())), preferred_element_type=jnp.float32
    )


def column_of(run_row, width):
    return jnp.transpose(jnp.broadcast_to(run_row, (width, run_row.shape[1])))


def inner_part(values, keys_in, queries, run_row, run_col, skip):
    length, width = values.shape
    half = length // 2
    lower = lax.broadcasted_iota(jnp.int32, (half, half), 0) >= lax.broadcasted_iota(
        jnp.int32, (half, half), 1
    )
    reps = half // width

    def decay(rows, columns, masked):
        left = jnp.concatenate([run_col[rows]] * reps, axis=1) if reps > 1 else run_col[rows]
        spread = left - run_row[:, columns]
        return jnp.exp(jnp.where(lower, spread, -jnp.inf) if masked else spread)

    top, bottom = slice(0, half), slice(half, length)
    scores_top = dot_nt(queries[top], keys_in[top])
    scores_bottom = dot_nt(queries[bottom], keys_in)
    mix_top = (scores_top * decay(top, top, True)).astype(jnp.bfloat16)
    mix_bottom = jnp.concatenate(
        [
            (scores_bottom[:, top] * decay(bottom, top, False)).astype(jnp.bfloat16),
            (scores_bottom[:, bottom] * decay(bottom, bottom, True)).astype(jnp.bfloat16),
        ],
        axis=1,
    )
    inner = jnp.concatenate(
        [
            jnp.dot(mix_top, values[top], preferred_element_type=jnp.float32),
            jnp.dot(mix_bottom, values, preferred_element_type=jnp.float32),
        ],
        axis=0,
    )
    return inner + skip * values.astype(jnp.float32)


def state_part(values, keys_in, run_col):
    last = run_col[run_col.shape[0] - 1 :, :]
    weighted = (keys_in.astype(jnp.float32) * jnp.exp(last - run_col)).astype(jnp.bfloat16)
    return dot_tn(weighted, values)


def outer_part(queries, run_col, state):
    outer = jnp.dot(queries, state.astype(jnp.bfloat16), preferred_element_type=jnp.float32)
    return jnp.exp(run_col) * outer


def advanced(state, run_col, update):
    return jnp.exp(run_col[run_col.shape[0] - 1 :, :]) * state + update


def norm_factor(raw):
    return lax.rsqrt(jnp.mean(raw * raw, axis=1, keepdims=True) + 1e-05)


def fused_kernel(parts, heads, *refs):
    values, keys_in, queries, steps, w_values, w_keys = refs[:6]
    small_in, out = refs[6:14], refs[14]
    v_buf, k_buf, q_buf, step_buf, wv_buf, wk_buf = refs[15:21]
    small = refs[21:29]
    w_step, gain_first, gain_second = small[:3]
    rates_first, skip_first, step_bias, rates_second, skip_second = small[3:]
    stage_raw, stage_state, raw_buf, state_buf, out_maps, out_steps = refs[29:35]
    first_buf, turn_buf, send_buf = refs[35:38]
    own_sem, unit_sem, in_send, in_recv, out_own, out_send, out_recv = refs[38:]
    me = lax.axis_index("seq")
    length, width = v_buf.shape[1:]
    rows_all, cols_here = send_buf.shape[1:3]
    rows_here = rows_all // parts
    my_slab, my_head = me // heads, lax.rem(me, heads)
    turn = jnp.where(me < parts // 2, parts - 1, 1)

    def peer(hop):
        return lax.rem(me + turn * hop, parts)

    def lanes(head):
        return pl.ds(pl.multiple_of(head * width, width), width)

    def unit_of(array, unit):
        return array.at[unit // heads, :, lanes(lax.rem(unit, heads))]

    barrier = pltpu.get_barrier_semaphore()
    for hop in range(1, parts):
        pl.semaphore_signal(
            barrier,
            inc=1,
            device_id={"seq": peer(hop)},
            device_id_type=pl.DeviceIdType.MESH,
        )
    own = [
        pltpu.make_async_copy(steps, step_buf, own_sem.at[0]),
        pltpu.make_async_copy(w_values.at[my_head], wv_buf, own_sem.at[1]),
        pltpu.make_async_copy(w_keys.at[my_head], wk_buf, own_sem.at[2]),
    ]
    for index, (src, dst) in enumerate(zip(small_in, small)):
        own.append(pltpu.make_async_copy(src, dst, own_sem.at[3 + index]))
    for unit in range(parts):
        for kind, (src, dst) in enumerate(((keys_in, k_buf), (queries, q_buf), (values, v_buf))):
            own.append(
                pltpu.make_async_copy(unit_of(src, unit), dst.at[unit], unit_sem.at[kind, unit])
            )
    for copy in own:
        copy.start()
    pl.semaphore_wait(barrier, parts - 1)

    def remote(kind, hop, src, dst, target, slot):
        return pltpu.make_async_remote_copy(
            src_ref=src,
            dst_ref=dst,
            send_sem=in_send.at[kind, hop],
            recv_sem=in_recv.at[kind, slot],
            device_id={"seq": target},
            device_id_type=pl.DeviceIdType.MESH,
        )

    def steps_copy(hop, target):
        src = steps.at[target // heads]
        return remote(0, hop, src, out_steps.at[me], target, me)

    def maps_copy(hop, target):
        return remote(1, hop, unit_of(queries, target), out_maps.at[me], target, me)

    def state_copy(hop, target):
        return remote(2, hop, stage_state.at[hop], state_buf.at[me], target, me)

    def raw_copy(hop, target):
        return remote(3, hop, stage_raw.at[hop], raw_buf.at[me], target, me)

    @pl.when(me > 0)
    def _():
        for hop in range(1, parts):
            steps_copy(hop, peer(hop)).start()
            maps_copy(hop, peer(hop)).start()

    upper = jnp.where(
        lax.broadcasted_iota(jnp.int32, (length, length), 0)
        <= lax.broadcasted_iota(jnp.int32, (length, length), 1),
        1.0,
        0.0,
    ).astype(jnp.bfloat16)

    for copy in own:
        copy.wait()

    def pick(head, select):
        chosen = select(0)
        for index in range(1, heads):
            chosen = jnp.where(head == index, select(index), chosen)
        return chosen

    def gain_of(gain, head):
        return pick(head, lambda h: gain[:, h * width : (h + 1) * width])

    step_row = pick(my_head, lambda h: w_step[...].astype(jnp.float32)[h : h + 1, :])
    step_rows = jnp.broadcast_to(step_row, (16, width)).astype(jnp.bfloat16)
    gain_one, gain_two = gain_of(gain_first, my_head), gain_of(gain_second, my_head)
    skip_two = skip_second[my_head]

    def row_of(step_rows_one, rate):
        return cumsum_rows(jnp.broadcast_to(-rate * step_rows_one, (8, length)), upper)[0:1]

    for hop in (*range(1, parts), 0):
        unit = peer(hop)
        head = lax.rem(unit, heads)
        run_row = row_of(step_buf[unit // heads, pl.ds(head, 1), :], rates_first[head])
        run_col = column_of(run_row, width)
        values_one, keys_one, queries_one = v_buf[unit], k_buf[unit], q_buf[unit]
        update = state_part(values_one, keys_one, run_col).astype(jnp.bfloat16)
        if hop:
            stage_state[hop] = update

            @pl.when(me < parts - 1)
            def _():
                state_copy(hop, unit).start()
        else:
            state_buf[me] = update
        raw = inner_part(values_one, keys_one, queries_one, run_row, run_col, skip_first[head])
        scale = norm_factor(raw) * gain_of(gain_first, head)
        sent = (raw * jnp.where(me == 0, scale, 1.0)).astype(jnp.bfloat16)
        if hop:
            stage_raw[hop] = sent
            raw_copy(hop, unit).start()
        else:
            raw_buf[me] = sent

    def await_from(block, kind, src, dst):
        @pl.when(me != block)
        def _():
            remote(kind, 0, src, dst.at[block], block, block).wait_recv()

    state = None
    for block in range(parts):
        if block:
            await_from(block, 0, steps.at[0], out_steps)
            await_from(block, 1, q_buf.at[0], out_maps)
            mine = me == block
            step_one = jnp.where(
                mine,
                step_buf[my_slab, pl.ds(my_head, 1), :],
                out_steps[block, pl.ds(my_head, 1), :],
            )
            run_col = column_of(row_of(step_one, rates_first[my_head]), width)
            maps_one = jnp.where(mine, q_buf[me], out_maps[block])
            raw_add = outer_part(maps_one, run_col, state)
        await_from(block, 3, stage_raw.at[0], raw_buf)
        raw = raw_buf[block].astype(jnp.float32)
        if block:
            raw = raw + raw_add
            raw = (raw * norm_factor(raw) * gain_one).astype(jnp.bfloat16).astype(jnp.float32)
        first_buf[pl.ds(block * length, length), :] = raw
        if block < parts - 1:
            await_from(block, 2, stage_state.at[0], state_buf)
            update = state_buf[block].astype(jnp.float32)
            state = advanced(state, run_col, update) if block else update

    sends = []
    state = None
    for block in range(parts):
        columns = jnp.concatenate(
            [
                first_buf[pl.ds(block * cols_here + col, rows_all, stride=rows_all), :]
                for col in range(cols_here)
            ],
            axis=0,
        ).astype(jnp.bfloat16)
        values_two = jnp.dot(
            columns, wv_buf[...], preferred_element_type=jnp.float32
        ).astype(jnp.bfloat16)
        keys_two = jnp.dot(columns, wk_buf[...], preferred_element_type=jnp.float32).astype(
            jnp.bfloat16
        )
        pre = dot_nt(step_rows, columns)[0:8].astype(jnp.bfloat16).astype(jnp.float32)
        shifted = pre + step_bias[my_head]
        soft = jnp.maximum(shifted, 0.0) + jnp.log1p(jnp.exp(-jnp.abs(shifted)))
        run_row = cumsum_rows(-rates_second[my_head] * soft, upper)[0:1]
        run_col = column_of(run_row, width)
        half = keys_two.shape[1] // 2
        keys_now, queries_now = keys_two[:, :half], keys_two[:, half:]
        raw = inner_part(values_two, keys_now, queries_now, run_row, run_col, skip_two)
        if block:
            raw = raw + outer_part(queries_now, run_col, state)
        if block < parts - 1:
            update = state_part(values_two, keys_now, run_col)
            state = advanced(state, run_col, update) if block else update
        normed = (raw * norm_factor(raw) * gain_two).astype(jnp.bfloat16)
        turn_buf[block] = normed.astype(jnp.float32)
        for row in range(rows_all):
            total = (
                first_buf[pl.ds(row * rows_all + block * cols_here, cols_here), :]
                + turn_buf[block, pl.ds(row, cols_here, stride=rows_all), :]
            )
            send_buf[block, row] = total.astype(jnp.bfloat16)

        def home(owner):
            return send_buf.at[block, pl.ds(owner * rows_here, rows_here)]

        def place(owner):
            slab, head = owner // heads, lax.rem(owner, heads)
            return out.at[slab, :, pl.ds(block * cols_here, cols_here), lanes(head)]

        for hop in range(1, parts):
            target = peer(hop)
            copy = pltpu.make_async_remote_copy(
                src_ref=home(target),
                dst_ref=place(me),
                send_sem=out_send.at[block, hop],
                recv_sem=out_recv.at[block, me],
                device_id={"seq": target},
                device_id_type=pl.DeviceIdType.MESH,
            )
            copy.start()
            sends.append(copy)
        pltpu.make_async_copy(home(me), place(me), out_own.at[block]).start()

    for block in range(parts):
        def place(owner):
            slab, head = owner // heads, lax.rem(owner, heads)
            return out.at[slab, :, pl.ds(block * cols_here, cols_here), lanes(head)]

        mine = send_buf.at[block, pl.ds(me * rows_here, rows_here)]
        pltpu.make_async_copy(mine, place(me), out_own.at[block]).wait()
        for hop in range(1, parts):
            source = lax.rem(me + hop, parts)
            pltpu.make_async_remote_copy(
                src_ref=mine,
                dst_ref=place(source),
                send_sem=out_send.at[block, 0],
                recv_sem=out_recv.at[block, source],
                device_id={"seq": source},
                device_id_type=pl.DeviceIdType.MESH,
            ).wait_recv()
    for copy in sends:
        copy.wait_send()
    for hop in range(1, parts):
        raw_copy(hop, peer(hop)).wait_send()

    @pl.when(me > 0)
    def _():
        for hop in range(1, parts):
            steps_copy(hop, peer(hop)).wait_send()
            maps_copy(hop, peer(hop)).wait_send()

    @pl.when(me < parts - 1)
    def _():
        for hop in range(1, parts):
            state_copy(hop, peer(hop)).wait_send()


def local_fused(
    parts,
    values_first,
    keys_first,
    queries_first,
    steps_first,
    rates_first,
    skip_first,
    gain_first,
    w_values,
    w_keys,
    w_step,
    step_bias,
    rates_second,
    skip_second,
    gain_second,
):
    slab_count, length, feat_width = values_first.shape
    heads = rates_first.shape[0]
    width = feat_width // heads
    grid_side = math.isqrt(parts * length)
    rows_here, cols_here = grid_side // parts, length // grid_side
    anywhere = pl.BlockSpec(memory_space=pl.ANY)
    dma = pltpu.SemaphoreType.DMA
    mixed = pl.pallas_call(
        functools.partial(fused_kernel, parts, heads),
        out_shape=jax.ShapeDtypeStruct(
            (slab_count, rows_here, grid_side, feat_width), jnp.bfloat16
        ),
        in_specs=[anywhere] * 14,
        out_specs=pl.BlockSpec(memory_space=pltpu.VMEM),
        scratch_shapes=[
            pltpu.VMEM((parts, length, width), jnp.bfloat16),
            pltpu.VMEM((parts, length, width), jnp.bfloat16),
            pltpu.VMEM((parts, length, width), jnp.bfloat16),
            pltpu.VMEM(steps_first.shape, jnp.float32),
            pltpu.VMEM(w_values.shape[1:], jnp.bfloat16),
            pltpu.VMEM(w_keys.shape[1:], jnp.bfloat16),
            pltpu.VMEM(w_step.shape, jnp.bfloat16),
            pltpu.VMEM((1, feat_width), jnp.float32),
            pltpu.VMEM((1, feat_width), jnp.float32),
        ]
        + [pltpu.SMEM((heads,), jnp.float32)] * 5
        + [
            pltpu.VMEM((parts, length, width), jnp.bfloat16),
            pltpu.VMEM((parts, width, width), jnp.bfloat16),
            pltpu.VMEM((parts, length, width), jnp.bfloat16),
            pltpu.VMEM((parts, width, width), jnp.bfloat16),
            pltpu.VMEM((parts, length, width), jnp.bfloat16),
            pltpu.VMEM((parts, heads, length), jnp.float32),
            pltpu.VMEM((parts * length, width), jnp.float32),
            pltpu.VMEM((parts, length, width), jnp.float32),
            pltpu.VMEM((parts, grid_side, cols_here, width), jnp.bfloat16),
            dma((11,)),
            dma((3, parts)),
            dma((4, parts)),
            dma((4, parts)),
            dma((parts,)),
            dma((parts, parts)),
            dma((parts, parts)),
        ],
        compiler_params=pltpu.CompilerParams(
            collective_id=0, has_side_effects=True, vmem_limit_bytes=VMEM_GRANT
        ),
    )(
        *(
            pltpu.with_memory_space_constraint(array, pltpu.HBM)
            for array in (
                values_first,
                keys_first,
                queries_first,
                steps_first,
                w_values,
                w_keys,
                w_step,
                gain_first.reshape(1, -1),
                gain_second.reshape(1, -1),
                rates_first,
                skip_first,
                step_bias,
                rates_second,
                skip_second,
            )
        )
    )
    return mixed.reshape(values_first.shape)


def fits_fused(parts, args):
    values, w_values, w_keys = args[0], args[7], args[8]
    slab_count, length, feat_width = values.shape
    heads = args[4].shape[0]
    side = math.isqrt(parts * length)
    return (
        slab_count * heads == parts
        and length <= BLOCK
        and length % 256 == 0
        and side * side == parts * length
        and side % parts == 0
        and length % side == 0
        and (length // side) % 8 == 0
        and feat_width // heads == 128
        and w_values.shape[1:] == (128, 128)
        and w_keys.shape[1:] == (128, 256)
    )


def solution(mesh):
    parts = mesh.shape["seq"]

    def chosen(*args):
        if fits_fused(parts, args):
            return local_fused(parts, *args)
        return local(*args)

    placed = (
        P("slab", "seq", "head"),
        P("slab", "seq", "head"),
        P("slab", "seq", "head"),
        P("slab", "head", "seq"),
        P("head"),
        P("head"),
        P("head"),
        P("head", None, None),
        P("head", None, None),
        P("head", None),
        P("head"),
        P("head"),
        P("head"),
        P("head"),
    )
    return jax.shard_map(
        chosen, mesh=mesh, in_specs=placed, out_specs=P("slab", "seq", "head"), check_vma=False
    )
```

```python
import functools
import math

import jax
import jax.numpy as jnp
from jax import lax
from jax.experimental import pallas as pl
from jax.experimental.pallas import tpu as pltpu
from jax.sharding import PartitionSpec as P

N = 128
BLOCK = 256
ROWS_DEV = 8
VMEM_GRANT = 16 << 20


def block_terms(values, keys_in, queries, log_decay, block_len):
    slab_count, length, feat_width = values.shape
    head_count = log_decay.shape[1]
    blocks = length // block_len
    value_blocks = values.reshape(
        slab_count, blocks, block_len, head_count, feat_width // head_count
    )
    key_blocks = keys_in.reshape(
        slab_count, blocks, block_len, head_count, keys_in.shape[2] // head_count
    )
    query_blocks = queries.reshape(
        slab_count, blocks, block_len, head_count, queries.shape[2] // head_count
    )
    running = jnp.cumsum(log_decay.reshape(slab_count, head_count, blocks, block_len), axis=3)
    running_sc = jnp.transpose(running, (0, 2, 1, 3))
    running_pos = jnp.transpose(running, (0, 2, 3, 1))
    scores = jnp.einsum(
        "scihn,scjhn->schij", query_blocks, key_blocks, preferred_element_type=jnp.float32
    )
    row_ids = lax.broadcasted_iota(jnp.int32, (block_len, block_len), 0)
    col_ids = lax.broadcasted_iota(jnp.int32, (block_len, block_len), 1)
    spread = running_sc[..., :, None] - running_sc[..., None, :]
    decays = jnp.exp(jnp.where(row_ids >= col_ids, spread, -jnp.inf))
    mixing = (scores * decays).astype(jnp.bfloat16)
    inner_sum = jnp.einsum(
        "schij,scjhp->scihp", mixing, value_blocks, preferred_element_type=jnp.float32
    )
    to_end = jnp.exp(running_pos[:, :, -1:, :] - running_pos)
    weighted = (key_blocks * to_end[..., None]).astype(jnp.bfloat16)
    local_states = jnp.einsum(
        "scjhn,scjhp->schnp", weighted, value_blocks, preferred_element_type=jnp.float32
    )
    block_logs = running_sc[..., -1]
    return (value_blocks, query_blocks, running_pos, inner_sum, local_states, block_logs)


def entry_states(local_states, block_logs):

    def advance(carried, entry_item):
        update, log_total = entry_item
        return (jnp.exp(log_total)[..., None, None] * carried + update, carried)

    start_state = jnp.zeros(local_states.shape[:1] + local_states.shape[2:], jnp.float32)
    final_state, entries = lax.scan(
        advance, start_state, (jnp.moveaxis(local_states, 1, 0), jnp.moveaxis(block_logs, 1, 0))
    )
    return (final_state, jnp.moveaxis(entries, 0, 1))


def carry_into(final_state, device_log):
    log_totals = lax.all_gather(device_log[None], "seq", axis=0, tiled=True)
    my_index = lax.axis_index("seq")
    ranks_all = lax.iota(jnp.int32, log_totals.shape[0])
    between = jnp.logical_and(
        ranks_all[None, :] > ranks_all[:, None], ranks_all[None, :] < my_index
    ).astype(jnp.float32)
    span_logs = jnp.einsum("dk,ksh->dsh", between, log_totals, precision=lax.Precision.HIGHEST)
    weights = jnp.where((ranks_all < my_index)[:, None, None], jnp.exp(span_logs), 0.0)
    return jnp.sum(
        weights[..., None, None] * lax.all_gather(final_state[None], "seq", axis=0, tiled=True),
        axis=0,
    )


def selective_scan(values, keys_in, queries, log_decay, skip, gain):
    block_len = min(BLOCK, values.shape[1])
    value_blocks, query_blocks, running_pos, inner_sum, local_states, block_logs = block_terms(
        values, keys_in, queries, log_decay, block_len
    )
    final_state, entries = entry_states(local_states, block_logs)
    carried = carry_into(final_state, jnp.sum(block_logs, axis=1))
    before = jnp.cumsum(block_logs, axis=1) - block_logs
    states = (entries + jnp.exp(before)[..., None, None] * carried[:, None]).astype(jnp.bfloat16)
    outer_sum = jnp.einsum(
        "scihn,schnp->scihp", query_blocks, states, preferred_element_type=jnp.float32
    )
    raw_out = (
        inner_sum
        + outer_sum * jnp.exp(running_pos)[..., None]
        + skip[:, None] * value_blocks.astype(jnp.float32)
    )
    scaled = raw_out * lax.rsqrt(jnp.mean(raw_out * raw_out, axis=-1, keepdims=True) + 1e-05)
    normed = (scaled * gain.reshape(skip.shape[0], -1)).astype(jnp.bfloat16)
    return normed.reshape(normed.shape[0], -1, normed.shape[3] * normed.shape[4])


def project_rows(features, w_values, w_keys, w_step):
    slab_count, length, feat_width = features.shape
    head_count = w_values.shape[0]
    split_feat = features.reshape(slab_count, length, head_count, feat_width // head_count)
    values_two = jnp.einsum(
        "slhp,hpk->slhk", split_feat, w_values, preferred_element_type=jnp.float32
    ).astype(jnp.bfloat16)
    keys_two = jnp.einsum(
        "slhp,hpk->slhk", split_feat, w_keys, preferred_element_type=jnp.float32
    ).astype(jnp.bfloat16)
    step_pre = jnp.einsum(
        "slhp,hp->slh", split_feat, w_step, preferred_element_type=jnp.float32
    ).astype(jnp.bfloat16)
    return (values_two, keys_two, step_pre)


def second_scan(values_two, keys_two, step_pre, step_bias, rates_second, skip_second, gain_second):
    slab_count, length, head_count, key_width = keys_two.shape
    step_size = jax.nn.softplus(step_pre.astype(jnp.float32) + step_bias)
    log_decay = -rates_second[None, :, None] * jnp.transpose(step_size, (0, 2, 1))
    return selective_scan(
        values_two.reshape(slab_count, length, -1),
        keys_two[..., :N].reshape(slab_count, length, -1),
        keys_two[..., N:].reshape(slab_count, length, -1),
        log_decay,
        skip_second,
        gain_second,
    )


def columns_from(received):
    slab_count, rows_all, cols_here, last_width = received.shape
    return jnp.transpose(received, (0, 2, 1, 3)).reshape(
        slab_count, cols_here * rows_all, last_width
    )


def local(
    values_first,
    keys_first,
    queries_first,
    steps_first,
    rates_first,
    skip_first,
    gain_first,
    w_values,
    w_keys,
    w_step,
    step_bias,
    rates_second,
    skip_second,
    gain_second,
):
    log_first = -rates_first[None, :, None] * steps_first
    first_out = selective_scan(
        values_first, keys_first, queries_first, log_first, skip_first, gain_first
    )
    slab_count, length, feat_width = first_out.shape
    home_grid = first_out.reshape(slab_count, ROWS_DEV, length // ROWS_DEV, feat_width)
    received = lax.all_to_all(home_grid, "seq", split_axis=2, concat_axis=1, tiled=True)
    rows_all = received.shape[1]
    cols_here = received.shape[2]
    values_two, keys_two, step_pre = project_rows(columns_from(received), w_values, w_keys, w_step)
    result = second_scan(
        values_two, keys_two, step_pre, step_bias, rates_second, skip_second, gain_second
    )
    column_out = result.reshape(received.shape[0], cols_here, rows_all, result.shape[2])
    home_back = lax.all_to_all(column_out, "seq", split_axis=2, concat_axis=1, tiled=True)
    second_home = jnp.transpose(home_back, (0, 2, 1, 3)).reshape(slab_count, length, feat_width)
    return (first_out.astype(jnp.float32) + second_home.astype(jnp.float32)).astype(jnp.bfloat16)


def cumsum_rows(rows, upper):
    high = rows.astype(jnp.bfloat16).astype(jnp.float32)
    rest = rows - high
    mid = rest.astype(jnp.bfloat16).astype(jnp.float32)
    low = rest - mid
    count = rows.shape[0]
    stacked = jnp.concatenate([high, mid, low, jnp.zeros_like(low)], axis=0).astype(jnp.bfloat16)
    sums = jnp.dot(stacked, upper, preferred_element_type=jnp.float32)
    return sums[:count] + sums[count : 2 * count] + sums[2 * count : 3 * count]


def dot_nt(left, right):
    return lax.dot_general(
        left, right, (((1,), (1,)), ((), ())), preferred_element_type=jnp.float32
    )


def dot_tn(left, right):
    return lax.dot_general(
        left, right, (((0,), (0,)), ((), ())), preferred_element_type=jnp.float32
    )


def column_of(run_row, width):
    return jnp.transpose(jnp.broadcast_to(run_row, (width, run_row.shape[1])))


def inner_part(values, keys_in, queries, run_row, run_col, skip):
    length, width = values.shape
    half = length // 2
    lower = lax.broadcasted_iota(jnp.int32, (half, half), 0) >= lax.broadcasted_iota(
        jnp.int32, (half, half), 1
    )
    reps = half // width

    def decay(rows, columns, masked):
        left = jnp.concatenate([run_col[rows]] * reps, axis=1) if reps > 1 else run_col[rows]
        spread = left - run_row[:, columns]
        return jnp.exp(jnp.where(lower, spread, -jnp.inf) if masked else spread)

    top, bottom = slice(0, half), slice(half, length)
    scores_top = dot_nt(queries[top], keys_in[top])
    scores_bottom = dot_nt(queries[bottom], keys_in)
    mix_top = (scores_top * decay(top, top, True)).astype(jnp.bfloat16)
    mix_bottom = jnp.concatenate(
        [
            (scores_bottom[:, top] * decay(bottom, top, False)).astype(jnp.bfloat16),
            (scores_bottom[:, bottom] * decay(bottom, bottom, True)).astype(jnp.bfloat16),
        ],
        axis=1,
    )
    inner = jnp.concatenate(
        [
            jnp.dot(mix_top, values[top], preferred_element_type=jnp.float32),
            jnp.dot(mix_bottom, values, preferred_element_type=jnp.float32),
        ],
        axis=0,
    )
    return inner + skip * values.astype(jnp.float32)


def state_part(values, keys_in, run_col):
    last = run_col[run_col.shape[0] - 1 :, :]
    weighted = (keys_in.astype(jnp.float32) * jnp.exp(last - run_col)).astype(jnp.bfloat16)
    return dot_tn(weighted, values)


def outer_part(queries, run_col, state):
    outer = jnp.dot(queries, state.astype(jnp.bfloat16), preferred_element_type=jnp.float32)
    return jnp.exp(run_col) * outer


def advanced(state, run_col, update):
    return jnp.exp(run_col[run_col.shape[0] - 1 :, :]) * state + update


def norm_factor(raw):
    return lax.rsqrt(jnp.mean(raw * raw, axis=1, keepdims=True) + 1e-05)


def fused_kernel(parts, heads, *refs):
    values, keys_in, queries, steps, w_values, w_keys = refs[:6]
    small_in, out = refs[6:14], refs[14]
    v_buf, k_buf, q_buf, step_buf, wv_buf, wk_buf = refs[15:21]
    small = refs[21:29]
    w_step, gain_first, gain_second = small[:3]
    rates_first, skip_first, step_bias, rates_second, skip_second = small[3:]
    stage_raw, stage_state, raw_buf, state_buf, out_maps, out_steps = refs[29:35]
    first_buf, turn_buf, send_buf = refs[35:38]
    own_sem, unit_sem, in_send, in_recv, out_own, out_send, out_recv = refs[38:]
    me = lax.axis_index("seq")
    length, width = v_buf.shape[1:]
    rows_all, cols_here = send_buf.shape[1:3]
    rows_here = rows_all // parts
    my_slab, my_head = me // heads, lax.rem(me, heads)
    turn = jnp.where(me < parts // 2, parts - 1, 1)

    def peer(hop):
        return lax.rem(me + turn * hop, parts)

    def lanes(head):
        return pl.ds(pl.multiple_of(head * width, width), width)

    def unit_of(array, unit):
        return array.at[unit // heads, :, lanes(lax.rem(unit, heads))]

    barrier = pltpu.get_barrier_semaphore()
    for hop in range(1, parts):
        pl.semaphore_signal(
            barrier,
            inc=1,
            device_id={"seq": peer(hop)},
            device_id_type=pl.DeviceIdType.MESH,
        )
    own = [
        pltpu.make_async_copy(steps, step_buf, own_sem.at[0]),
        pltpu.make_async_copy(w_values.at[my_head], wv_buf, own_sem.at[1]),
        pltpu.make_async_copy(w_keys.at[my_head], wk_buf, own_sem.at[2]),
    ]
    for index, (src, dst) in enumerate(zip(small_in, small)):
        own.append(pltpu.make_async_copy(src, dst, own_sem.at[3 + index]))
    for unit in range(parts):
        for kind, (src, dst) in enumerate(((keys_in, k_buf), (queries, q_buf), (values, v_buf))):
            own.append(
                pltpu.make_async_copy(unit_of(src, unit), dst.at[unit], unit_sem.at[kind, unit])
            )
    for copy in own:
        copy.start()
    pl.semaphore_wait(barrier, parts - 1)

    def remote(kind, hop, src, dst, target, slot):
        return pltpu.make_async_remote_copy(
            src_ref=src,
            dst_ref=dst,
            send_sem=in_send.at[kind, hop],
            recv_sem=in_recv.at[kind, slot],
            device_id={"seq": target},
            device_id_type=pl.DeviceIdType.MESH,
        )

    def steps_copy(hop, target):
        src = steps.at[target // heads]
        return remote(0, hop, src, out_steps.at[me], target, me)

    def maps_copy(hop, target):
        return remote(1, hop, unit_of(queries, target), out_maps.at[me], target, me)

    def state_copy(hop, target):
        return remote(2, hop, stage_state.at[hop], state_buf.at[me], target, me)

    def raw_copy(hop, target):
        return remote(3, hop, stage_raw.at[hop], raw_buf.at[me], target, me)

    @pl.when(me > 0)
    def _():
        for hop in range(1, parts):
            maps_copy(hop, peer(hop)).start()
        for hop in range(1, parts):
            steps_copy(hop, peer(hop)).start()

    upper = jnp.where(
        lax.broadcasted_iota(jnp.int32, (length, length), 0)
        <= lax.broadcasted_iota(jnp.int32, (length, length), 1),
        1.0,
        0.0,
    ).astype(jnp.bfloat16)

    for copy in own:
        copy.wait()

    def pick(head, select):
        chosen = select(0)
        for index in range(1, heads):
            chosen = jnp.where(head == index, select(index), chosen)
        return chosen

    def gain_of(gain, head):
        return pick(head, lambda h: gain[:, h * width : (h + 1) * width])

    step_row = pick(my_head, lambda h: w_step[...].astype(jnp.float32)[h : h + 1, :])
    step_rows = jnp.broadcast_to(step_row, (16, width)).astype(jnp.bfloat16)
    gain_one, gain_two = gain_of(gain_first, my_head), gain_of(gain_second, my_head)
    skip_two = skip_second[my_head]

    def row_of(step_rows_one, rate):
        return cumsum_rows(jnp.broadcast_to(-rate * step_rows_one, (8, length)), upper)[0:1]

    for hop in (*range(1, parts), 0):
        unit = peer(hop)
        head = lax.rem(unit, heads)
        run_row = row_of(step_buf[unit // heads, pl.ds(head, 1), :], rates_first[head])
        run_col = column_of(run_row, width)
        values_one, keys_one, queries_one = v_buf[unit], k_buf[unit], q_buf[unit]
        update = state_part(values_one, keys_one, run_col).astype(jnp.bfloat16)
        raw = inner_part(values_one, keys_one, queries_one, run_row, run_col, skip_first[head])
        scale = norm_factor(raw) * gain_of(gain_first, head)
        sent = (raw * jnp.where(me == 0, scale, 1.0)).astype(jnp.bfloat16)
        if hop:
            stage_raw[hop] = sent
            stage_state[hop] = update
            raw_copy(hop, unit).start()

            @pl.when(me < parts - 1)
            def _():
                state_copy(hop, unit).start()
        else:
            raw_buf[me] = sent
            state_buf[me] = update

    def await_from(block, kind, src, dst):
        @pl.when(me != block)
        def _():
            remote(kind, 0, src, dst.at[block], block, block).wait_recv()

    state = None
    for block in range(parts):
        if block:
            await_from(block, 0, steps.at[0], out_steps)
            await_from(block, 1, q_buf.at[0], out_maps)
            mine = me == block
            step_one = jnp.where(
                mine,
                step_buf[my_slab, pl.ds(my_head, 1), :],
                out_steps[block, pl.ds(my_head, 1), :],
            )
            run_col = column_of(row_of(step_one, rates_first[my_head]), width)
            maps_one = jnp.where(mine, q_buf[me], out_maps[block])
            raw_add = outer_part(maps_one, run_col, state)
        await_from(block, 3, stage_raw.at[0], raw_buf)
        raw = raw_buf[block].astype(jnp.float32)
        if block:
            raw = raw + raw_add
            raw = (raw * norm_factor(raw) * gain_one).astype(jnp.bfloat16).astype(jnp.float32)
        first_buf[pl.ds(block * length, length), :] = raw
        if block < parts - 1:
            await_from(block, 2, stage_state.at[0], state_buf)
            update = state_buf[block].astype(jnp.float32)
            state = advanced(state, run_col, update) if block else update

    sends = []
    state = None
    for block in range(parts):
        columns = jnp.concatenate(
            [
                first_buf[pl.ds(block * cols_here + col, rows_all, stride=rows_all), :]
                for col in range(cols_here)
            ],
            axis=0,
        ).astype(jnp.bfloat16)
        values_two = jnp.dot(
            columns, wv_buf[...], preferred_element_type=jnp.float32
        ).astype(jnp.bfloat16)
        keys_two = jnp.dot(columns, wk_buf[...], preferred_element_type=jnp.float32).astype(
            jnp.bfloat16
        )
        pre = dot_nt(step_rows, columns)[0:8].astype(jnp.bfloat16).astype(jnp.float32)
        shifted = pre + step_bias[my_head]
        soft = jnp.maximum(shifted, 0.0) + jnp.log1p(jnp.exp(-jnp.abs(shifted)))
        run_row = cumsum_rows(-rates_second[my_head] * soft, upper)[0:1]
        run_col = column_of(run_row, width)
        half = keys_two.shape[1] // 2
        keys_now, queries_now = keys_two[:, :half], keys_two[:, half:]
        raw = inner_part(values_two, keys_now, queries_now, run_row, run_col, skip_two)
        if block:
            raw = raw + outer_part(queries_now, run_col, state)
        normed = (raw * norm_factor(raw) * gain_two).astype(jnp.bfloat16)
        turn_buf[block] = normed.astype(jnp.float32)
        for row in range(rows_all):
            total = (
                first_buf[pl.ds(row * rows_all + block * cols_here, cols_here), :]
                + turn_buf[block, pl.ds(row, cols_here, stride=rows_all), :]
            )
            send_buf[block, row] = total.astype(jnp.bfloat16)

        def home(owner):
            return send_buf.at[block, pl.ds(owner * rows_here, rows_here)]

        def place(owner):
            slab, head = owner // heads, lax.rem(owner, heads)
            return out.at[slab, :, pl.ds(block * cols_here, cols_here), lanes(head)]

        for hop in range(1, parts):
            target = peer(hop)
            copy = pltpu.make_async_remote_copy(
                src_ref=home(target),
                dst_ref=place(me),
                send_sem=out_send.at[block, hop],
                recv_sem=out_recv.at[block, me],
                device_id={"seq": target},
                device_id_type=pl.DeviceIdType.MESH,
            )
            copy.start()
            sends.append(copy)
        pltpu.make_async_copy(home(me), place(me), out_own.at[block]).start()
        if block < parts - 1:
            update = state_part(values_two, keys_now, run_col)
            state = advanced(state, run_col, update) if block else update

    for block in range(parts):
        def place(owner):
            slab, head = owner // heads, lax.rem(owner, heads)
            return out.at[slab, :, pl.ds(block * cols_here, cols_here), lanes(head)]

        mine = send_buf.at[block, pl.ds(me * rows_here, rows_here)]
        pltpu.make_async_copy(mine, place(me), out_own.at[block]).wait()
        for hop in range(1, parts):
            source = lax.rem(me + hop, parts)
            pltpu.make_async_remote_copy(
                src_ref=mine,
                dst_ref=place(source),
                send_sem=out_send.at[block, 0],
                recv_sem=out_recv.at[block, source],
                device_id={"seq": source},
                device_id_type=pl.DeviceIdType.MESH,
            ).wait_recv()
    for copy in sends:
        copy.wait_send()
    for hop in range(1, parts):
        raw_copy(hop, peer(hop)).wait_send()

    @pl.when(me > 0)
    def _():
        for hop in range(1, parts):
            steps_copy(hop, peer(hop)).wait_send()
            maps_copy(hop, peer(hop)).wait_send()

    @pl.when(me < parts - 1)
    def _():
        for hop in range(1, parts):
            state_copy(hop, peer(hop)).wait_send()


def local_fused(
    parts,
    values_first,
    keys_first,
    queries_first,
    steps_first,
    rates_first,
    skip_first,
    gain_first,
    w_values,
    w_keys,
    w_step,
    step_bias,
    rates_second,
    skip_second,
    gain_second,
):
    slab_count, length, feat_width = values_first.shape
    heads = rates_first.shape[0]
    width = feat_width // heads
    grid_side = math.isqrt(parts * length)
    rows_here, cols_here = grid_side // parts, length // grid_side
    anywhere = pl.BlockSpec(memory_space=pl.ANY)
    dma = pltpu.SemaphoreType.DMA
    mixed = pl.pallas_call(
        functools.partial(fused_kernel, parts, heads),
        out_shape=jax.ShapeDtypeStruct(
            (slab_count, rows_here, grid_side, feat_width), jnp.bfloat16
        ),
        in_specs=[anywhere] * 14,
        out_specs=pl.BlockSpec(memory_space=pltpu.VMEM),
        scratch_shapes=[
            pltpu.VMEM((parts, length, width), jnp.bfloat16),
            pltpu.VMEM((parts, length, width), jnp.bfloat16),
            pltpu.VMEM((parts, length, width), jnp.bfloat16),
            pltpu.VMEM(steps_first.shape, jnp.float32),
            pltpu.VMEM(w_values.shape[1:], jnp.bfloat16),
            pltpu.VMEM(w_keys.shape[1:], jnp.bfloat16),
            pltpu.VMEM(w_step.shape, jnp.bfloat16),
            pltpu.VMEM((1, feat_width), jnp.float32),
            pltpu.VMEM((1, feat_width), jnp.float32),
        ]
        + [pltpu.SMEM((heads,), jnp.float32)] * 5
        + [
            pltpu.VMEM((parts, length, width), jnp.bfloat16),
            pltpu.VMEM((parts, width, width), jnp.bfloat16),
            pltpu.VMEM((parts, length, width), jnp.bfloat16),
            pltpu.VMEM((parts, width, width), jnp.bfloat16),
            pltpu.VMEM((parts, length, width), jnp.bfloat16),
            pltpu.VMEM((parts, heads, length), jnp.float32),
            pltpu.VMEM((parts * length, width), jnp.float32),
            pltpu.VMEM((parts, length, width), jnp.float32),
            pltpu.VMEM((parts, grid_side, cols_here, width), jnp.bfloat16),
            dma((11,)),
            dma((3, parts)),
            dma((4, parts)),
            dma((4, parts)),
            dma((parts,)),
            dma((parts, parts)),
            dma((parts, parts)),
        ],
        compiler_params=pltpu.CompilerParams(
            collective_id=0, has_side_effects=True, vmem_limit_bytes=VMEM_GRANT
        ),
    )(
        *(
            pltpu.with_memory_space_constraint(array, pltpu.HBM)
            for array in (
                values_first,
                keys_first,
                queries_first,
                steps_first,
                w_values,
                w_keys,
                w_step,
                gain_first.reshape(1, -1),
                gain_second.reshape(1, -1),
                rates_first,
                skip_first,
                step_bias,
                rates_second,
                skip_second,
            )
        )
    )
    return mixed.reshape(values_first.shape)


def fits_fused(parts, args):
    values, w_values, w_keys = args[0], args[7], args[8]
    slab_count, length, feat_width = values.shape
    heads = args[4].shape[0]
    side = math.isqrt(parts * length)
    return (
        slab_count * heads == parts
        and length <= BLOCK
        and length % 256 == 0
        and side * side == parts * length
        and side % parts == 0
        and length % side == 0
        and (length // side) % 8 == 0
        and feat_width // heads == 128
        and w_values.shape[1:] == (128, 128)
        and w_keys.shape[1:] == (128, 256)
    )


def solution(mesh):
    parts = mesh.shape["seq"]

    def chosen(*args):
        if fits_fused(parts, args):
            return local_fused(parts, *args)
        return local(*args)

    placed = (
        P("slab", "seq", "head"),
        P("slab", "seq", "head"),
        P("slab", "seq", "head"),
        P("slab", "head", "seq"),
        P("head"),
        P("head"),
        P("head"),
        P("head", None, None),
        P("head", None, None),
        P("head", None),
        P("head"),
        P("head"),
        P("head"),
        P("head"),
    )
    return jax.shard_map(
        chosen, mesh=mesh, in_specs=placed, out_specs=P("slab", "seq", "head"), check_vma=False
    )
```
